32 devices in a mesh: dp: 8 (over z, x), mp: 4 (over y, core).
Axes of the slice: x: 2, y: 2, z: 4, core: 2. Of those that a mesh axis runs over, the one named last changes fastest.
Arguments:
- conv_in: bfloat16 [16384, 1024], P('dp'), may hold values from -6 to 6
- conv_weight: bfloat16 [1024, 512], P(None, 'mp'), may hold values from -0.1875 to 0.1875
- feature_gain: float32 [512], replicated, may hold values from 0.1 to 1.9
- proj_weight: bfloat16 [512, 1024], replicated, may hold values from -0.25 to 0.25
- block_gain: float32 [1024], replicated, may hold values from 0.1 to 1.9
- w_in: bfloat16 [1024, 4096], P(None, 'mp'), may hold values from -0.1875 to 0.1875
- w_out: bfloat16 [1024, 4096], P(None, 'mp'), may hold values from -0.09375 to 0.09375
- cotangent: bfloat16 [16384, 1024], P('dp'), may hold values from -0.0625 to 0.0625
- send_index: int32 [16384], P('dp'), may hold values from 0 to 2047, as said below
- slot_valid: int32 [16384], P('dp'), may hold values from 0 to 1, as said below
Outputs:
- grad_conv_weight: float32 [1024, 512], P('dp', 'mp')
- grad_proj_weight: float32 [512, 1024], P('dp', 'mp')
- grad_w_in: float32 [1024, 4096], P('dp', 'mp')
- grad_w_out: float32 [1024, 4096], P('dp', 'mp')
The draws below stay inside these ranges and needn't reach their ends.
Inputs may be any that keep to these rules, and one draw needn't show every extreme that they name: `send_index`: the 2048 entries held by one index of dp are a permutation of 0 to 2047; entry e * 256 + j names the local frame sent to slot j of index e. `slot_valid`: slot j of the block from source s on index e is 1 exactly when the frame it receives lies inside the source's clips; a source's frames inside clips are its first ones, at least 512 of them, and some source has all 2048.
All inputs are finite; a program needn't handle non-finite values.
Results may differ from the reference program's by a relative error of at most 0.015.
Values may be sent and summed in bfloat16 or wider, within the bound.
A program may use at most 128 MiB of HBM per device.

```python
import jax
import jax.numpy as jnp
from jax import lax

C = 512
D = 1024
FF = 4096
FR = 2048
SLOT = 256
ROWS = 16384
N_DP = 8
N_MP = 4


def packing_plan(key):
    key_order, key_count, key_full = jax.random.split(jax.random.fold_in(key, 11), 3)
    orders = jax.vmap(lambda item: jax.random.permutation(item, FR))(jax.random.split(key_order, N_DP))
    counts = jax.random.randint(key_count, (N_DP,), FR // 4, FR + 1)
    full_sender = jax.random.randint(key_full, (), 0, N_DP)
    counts = jnp.where(jnp.arange(N_DP) == full_sender, FR, counts)
    return (orders.astype(jnp.int32), counts.astype(jnp.int32))


def draw_send_index(key, part):
    orders, counts = packing_plan(key)
    return orders.reshape(N_DP * FR).astype(jnp.int32)


def draw_slot_valid(key, part):
    orders, counts = packing_plan(key)
    inside = (orders < counts[:, None]).astype(jnp.int32)
    return jnp.transpose(inside.reshape(N_DP, N_DP, SLOT), (1, 0, 2)).reshape(N_DP * FR).astype(jnp.int32)


def spiked(drawn, own_key, source, target, blocks, factor):
    owner, partner = [(jnp.arange(drawn.shape[dim]) // (drawn.shape[dim] // blocks)).reshape([-1 if axis == dim else 1 for axis in range(drawn.ndim)]) for dim in (source, target)]
    chosen = jax.random.permutation(own_key, blocks)[partner]
    strong = (owner == chosen) | (owner == (partner + blocks // 2) % blocks)
    return jnp.where(strong, factor * drawn, drawn)


def level_of(key, shape, cuts, least, largest):
    def one(axis_at, parts):
        draws = jax.random.uniform(jax.random.fold_in(jax.random.fold_in(key, 6), axis_at), (parts,), jnp.float32, least / len(cuts), largest / len(cuts))
        return jnp.repeat(jnp.exp(draws), shape[axis_at] // parts).reshape((-1,) + (1,) * (len(shape) - axis_at - 1))

    level = one(*cuts[0])
    for cut in cuts[1:]:
        level = level * one(*cut)
    return level


def normal_values(own_key, extent, scale, most, cuts=(), kind=jnp.bfloat16):
    array = scale * jax.random.normal(own_key, extent, jnp.float32)
    if cuts:
        array = array * level_of(own_key, extent, cuts, -0.22, 0.18)
    return jnp.clip(array, -most, most).astype(kind)


def bell_draw_with(own_key, dims, spread, most, cuts, heavy, kind=jnp.bfloat16):
    result = spread * jax.random.normal(own_key, dims, jnp.float32)
    if cuts:
        result = result * level_of(own_key, dims, cuts, -0.22, 0.18)
    return jnp.clip(spiked(result, jax.random.fold_in(own_key, 3), *heavy), -most, most).astype(kind)


def setup_inputs(seed: int = 0) -> dict:
    streams_of = jax.random.split(jax.random.key(seed), 11)
    conv_in = normal_values(streams_of[0], (ROWS, 2 * C), 1.0, 6.0, ((0, 8),))
    conv_weight = normal_values(streams_of[1], (2 * C, C), (2 * C) ** -0.5, 0.1875, ((1, 4),))
    feature_gain = jnp.clip(1.0 + 0.18 * jax.random.normal(streams_of[2], (C,), jnp.float32), 0.1, 1.9)
    proj_weight = normal_values(streams_of[3], (C, D), C ** -0.5, 0.25)
    block_gain = jnp.clip(1.0 + 0.18 * jax.random.normal(streams_of[4], (D,), jnp.float32), 0.1, 1.9)
    w_in = normal_values(streams_of[5], (D, FF), D ** -0.5, 0.1875, ((1, 4),))
    w_out = normal_values(streams_of[6], (D, FF), FF ** -0.5, 0.09375, ((1, 4),))
    cotangent = bell_draw_with(streams_of[7], (ROWS, D), ((FR * N_DP) ** -0.5), 0.0625, ((0, 8),), (0, 1, 8, 2.0))
    send_index = draw_send_index(jax.random.fold_in(streams_of[10], 71), 0)
    slot_valid = draw_slot_valid(jax.random.fold_in(streams_of[10], 71), 0)
    return dict(conv_in=conv_in, conv_weight=conv_weight, feature_gain=feature_gain, proj_weight=proj_weight, block_gain=block_gain, w_in=w_in, w_out=w_out, cotangent=cotangent, send_index=send_index, slot_valid=slot_valid)


EPSILON = 1e-05
SQRT_HALF = 0.7071067811865476
INV_SQRT_TWO_PI = 0.3989422804014327

def gelu_exact(values):
    return 0.5 * values * (1.0 + lax.erf(values * SQRT_HALF))

def gelu_slope(values):
    return 0.5 * (1.0 + lax.erf(values * SQRT_HALF)) + values * INV_SQRT_TWO_PI * jnp.exp(-0.5 * values * values)

def normalize(values):
    row_mean = lax.optimization_barrier(jnp.mean(values, axis=-1, keepdims=True))
    centred = values - row_mean
    inv_std = lax.rsqrt(lax.optimization_barrier(jnp.mean(centred * centred, axis=-1, keepdims=True)) + EPSILON)
    return (centred * inv_std, inv_std)

def norm_back(upstream, normed, inv_std, gain_row):
    scaled = upstream * gain_row
    first_mean = lax.optimization_barrier(jnp.mean(scaled, axis=-1, keepdims=True))
    second_mean = lax.optimization_barrier(jnp.mean(scaled * normed, axis=-1, keepdims=True))
    return inv_std * (scaled - first_mean - normed * second_mean)

def contract_rows(left, right):
    return lax.dot_general(left, right, (((0,), (0,)), ((), ())), preferred_element_type=jnp.float32)

def contract_cols(left, right):
    return lax.dot_general(left, right, (((1,), (1,)), ((), ())), preferred_element_type=jnp.float32)

def reference(conv_in, conv_weight, feature_gain, proj_weight, block_gain, w_in, w_out, cotangent, send_index, slot_valid):
    pre_act = jnp.dot(conv_in, conv_weight, preferred_element_type=jnp.float32)
    features = gelu_exact(pre_act).astype(jnp.bfloat16)
    offsets = (jnp.arange(N_DP, dtype=jnp.int32) * FR).astype(jnp.int32)
    source = send_index.reshape(N_DP, N_DP, SLOT) + offsets[:, None, None]
    source = jnp.transpose(source, (1, 0, 2)).reshape(N_DP * FR).astype(jnp.int32)
    packed = features[source]
    slot_keep = slot_valid.astype(jnp.bfloat16)[:, None]
    block_width = FF // N_MP
    gain_feat = feature_gain.astype(jnp.float32)
    gain_block = block_gain.astype(jnp.float32)

    def group_step(totals, inputs):
        feat_rows, cot_rows, keep_rows = inputs
        feat_norm, feat_inv = normalize(feat_rows.astype(jnp.float32))
        feat_ln = (feat_norm * gain_feat).astype(jnp.bfloat16)
        hidden = jnp.dot(feat_ln, proj_weight, preferred_element_type=jnp.float32)
        hid_norm, hid_inv = normalize(hidden)
        hid_ln = (hid_norm * gain_block).astype(jnp.bfloat16)
        upward = jnp.dot(hid_ln, w_in, preferred_element_type=jnp.float32)
        active = gelu_exact(upward).astype(jnp.bfloat16)
        masked_cot = cot_rows * keep_rows
        grad_active = jnp.dot(masked_cot, w_out, preferred_element_type=jnp.float32)
        grad_upward = (grad_active * gelu_slope(upward)).astype(jnp.bfloat16)
        out_term = contract_rows(masked_cot, active)
        in_term = contract_rows(hid_ln, grad_upward)
        grad_normed = jnp.zeros(hidden.shape, jnp.float32)
        for block in range(N_MP):
            piece = contract_cols(grad_upward[:, block * block_width:(block + 1) * block_width], w_in[:, block * block_width:(block + 1) * block_width])
            rounded = lax.optimization_barrier(piece.astype(jnp.bfloat16))
            grad_normed = grad_normed + rounded.astype(jnp.float32)
        grad_hidden = (masked_cot.astype(jnp.float32) + norm_back(grad_normed, hid_norm, hid_inv, gain_block)).astype(jnp.bfloat16)
        proj_term = contract_rows(feat_ln, grad_hidden)
        grad_feat_ln = contract_cols(grad_hidden, proj_weight)
        grad_packed = norm_back(grad_feat_ln, feat_norm, feat_inv, gain_feat).astype(jnp.bfloat16)
        return ((totals[0] + proj_term, totals[1] + in_term, totals[2] + out_term), grad_packed)
    start = (jnp.zeros((C, D), jnp.float32), jnp.zeros((D, FF), jnp.float32), jnp.zeros((D, FF), jnp.float32))
    sums, grad_groups = lax.scan(group_step, start, (packed.reshape(N_DP, FR, C), cotangent.reshape(N_DP, FR, D), slot_keep.reshape(N_DP, FR, 1)))
    grad_proj_weight, grad_w_in, grad_w_out = sums
    grad_features = jnp.zeros((N_DP * FR, C), jnp.float32).at[source].add(grad_groups.reshape(N_DP * FR, C).astype(jnp.float32))
    grad_pre = (grad_features * gelu_slope(pre_act)).astype(jnp.bfloat16)
    grad_conv_weight = contract_rows(conv_in, grad_pre)
    return (grad_conv_weight, grad_proj_weight, grad_w_in, grad_w_out)
```

```python
import functools
import types

import jax
import jax.numpy as jnp
from jax import lax
from jax.experimental import pallas as pl
from jax.experimental.pallas import tpu as pltpu
from jax.sharding import PartitionSpec as P

EPSILON = 1e-05
SQRT_HALF = 0.7071067811865476
INV_SQRT_TWO_PI = 0.3989422804014327
VMEM_LIMIT = 67043328


def gelu_exact(values):
    return 0.5 * values * (1.0 + lax.erf(values * SQRT_HALF))


def gelu_slope(values):
    return 0.5 * (1.0 + lax.erf(values * SQRT_HALF)) + values * INV_SQRT_TWO_PI * jnp.exp(
        -0.5 * values * values
    )


def normalize(values):
    row_mean = jnp.mean(values, axis=-1, keepdims=True)
    centred = values - row_mean
    inv_std = lax.rsqrt(jnp.mean(centred * centred, axis=-1, keepdims=True) + EPSILON)
    return (centred * inv_std, inv_std)


def norm_back(upstream, normed, inv_std, gain_row):
    scaled = upstream * gain_row
    first_mean = jnp.mean(scaled, axis=-1, keepdims=True)
    second_mean = jnp.mean(scaled * normed, axis=-1, keepdims=True)
    return inv_std * (scaled - first_mean - normed * second_mean)


def contract_rows(left, right):
    return lax.dot_general(
        left, right, (((0,), (0,)), ((), ())), preferred_element_type=jnp.float32
    )


def contract_cols(left, right):
    return lax.dot_general(
        left, right, (((1,), (1,)), ((), ())), preferred_element_type=jnp.float32
    )


def start_copy(src, dst, send_sem, recv_sem, axis, index):
    copy = remote(src, dst, send_sem, recv_sem, axis, index)
    copy.start()
    return copy


def remote(src, dst, send_sem, recv_sem, axis, index):
    return pltpu.make_async_remote_copy(
        src_ref=src,
        dst_ref=dst,
        send_sem=send_sem,
        recv_sem=recv_sem,
        device_id={axis: index},
        device_id_type=pl.DeviceIdType.MESH,
    )


def greet(peers):
    barrier = pltpu.get_barrier_semaphore()
    for axis, index in peers:
        pl.semaphore_signal(
            barrier, inc=1, device_id={axis: index}, device_id_type=pl.DeviceIdType.MESH
        )
    pl.semaphore_wait(barrier, len(peers))


def block_of(index, size):
    return pl.ds(pl.multiple_of(index * size, size), size)


def loop(count, body):
    def step(t, carry):
        body(t)
        return carry

    lax.fori_loop(0, count, step, 0)


def step_kernel(parts, shards, names, *refs):
    r = types.SimpleNamespace(**dict(zip(names, refs)))
    outgoing, arrived, packed = r.outgoing, r.arrived, r.packed
    frames, width = outgoing.shape
    rows = frames // parts
    share = rows // shards
    fars = shards // 2
    group_rows = fars * share
    levels = parts.bit_length() - 1
    half = parts // 2
    w_in, w_out, proj, cot = r.w_in, r.w_out, r.proj, r.cot
    spare = r.spare
    d = lax.axis_index("dp")
    m = lax.axis_index("mp")
    side = lax.rem(m, 2)
    line = m // 2
    near = m + 1 - 2 * side
    piece = side * fars + line

    def load(src, dst, k):
        copy = pltpu.make_async_copy(src, dst, r.load_sem.at[k])
        copy.start()
        return copy

    load_w_out = load(r.w_out_hbm, w_out, 0)
    load_cot = load(r.cot_hbm, cot, 1)
    load_proj = load(r.proj_hbm, proj, 2)
    load_w_in = load(r.w_in_hbm, w_in, 3)

    def owner(k):
        total = 0
        for j in range(levels):
            bit = 2**j
            total = total + bit * lax.rem(lax.rem(d // bit, 2) + lax.rem(k // bit, 2), 2)
        return total

    def mate(j):
        bit = 2**j
        return d + bit - 2 * bit * lax.rem(d // bit, 2)

    def far(j):
        return lax.rem(m + 2 * j, shards)

    greet(
        [("dp", lax.rem(d + o, parts)) for o in range(1, parts)]
        + [("mp", lax.rem(m + o, shards)) for o in range(1, shards)]
    )

    def exchange(o):
        target = lax.rem(d + o, parts)
        return remote(
            outgoing.at[block_of(target, rows)],
            arrived.at[block_of(d, rows)],
            r.dp_send.at[o],
            r.dp_recv.at[o],
            "dp",
            target,
        )

    for o in range(1, parts):
        exchange(o).start()

    def source_of(o):
        return lax.rem(d - o + parts, parts)

    def place(o):
        return packed.at[block_of(source_of(o), rows), block_of(m, width)]

    def to_far(o, j, block):
        return remote(
            block, place(o), r.far_send.at[o, j], r.far_recv.at[o, j], "mp", far(j)
        )

    def to_near(o, block):
        return remote(block, place(o), r.near_send.at[o], r.near_recv.at[o], "mp", near)

    def keep(o, block):
        return pltpu.make_async_copy(block, place(o), r.keep_sem.at[o])

    def spread(o, block):
        for j in range(1, fars):
            to_far(o, j, block).start()
        to_near(o, block).start()
        keep(o, block).start()

    def relay(o):
        exchange(o).wait_recv()
        spread(o, arrived.at[block_of(source_of(o), rows)])

    def pass_on(o, j):
        col = block_of(lax.rem(m - 2 * j + shards, shards), width)
        part = packed.at[block_of(source_of(o), rows), col]
        return remote(part, part, r.pass_send.at[o, j], r.pass_recv.at[o, j], "mp", near)

    def hand_on(o):
        for j in range(1, fars):
            to_far(o, j, arrived.at[block_of(0, rows)]).wait_recv()
            pass_on(o, j).start()

    spread(0, outgoing.at[block_of(d, rows)])

    load_w_out.wait()
    load_cot.wait()

    def grad_active(t):
        span = block_of(t, rows)
        value = jnp.dot(cot[span, :], w_out[...], preferred_element_type=jnp.float32)
        spare[span, :] = (r.valid[span, :] * value).astype(jnp.bfloat16)
        now = (t + 1) // 2

        @pl.when(lax.rem(t, 2) == 1)
        def _():
            relay(now)
            hand_on(now - 1)

    loop(parts, grad_active)
    load_proj.wait()
    load_w_in.wait()

    def sum_near(s):
        return remote(
            r.normed_part.at[pl.ds(s * rows + (1 - side) * group_rows, group_rows)],
            r.near_in.at[s],
            r.sum_near_send.at[s],
            r.sum_near_recv.at[s],
            "mp",
            near,
        )

    def sum_far(s, j):
        return remote(
            r.staged.at[s, j],
            r.far_in.at[s, j],
            r.sum_far_send.at[s, j],
            r.sum_far_recv.at[s, j],
            "mp",
            far(j),
        )

    def pair_sum(s):
        sum_near(s).wait_recv()
        for j in range(fars):
            at = lax.rem(line + j, fars) * share
            mine = r.normed_part[pl.ds(pl.multiple_of(s * rows + side * group_rows + at, share), share), :]
            theirs = r.near_in[s, pl.ds(pl.multiple_of(at, share), share), :]
            total = mine.astype(jnp.float32) + theirs.astype(jnp.float32)
            if j:
                r.staged[s, j] = total.astype(jnp.bfloat16)
                sum_far(s, j).start()
            else:
                r.own_sum[s] = total

    def forward(o):
        s = source_of(o)
        span = block_of(s, rows)

        @pl.when(o + half + 1 < parts)
        def _():
            relay(o + half + 1)

        @pl.when(o + half < parts)
        def _():
            hand_on(o + half)

        to_near(o, arrived.at[block_of(0, rows)]).wait_recv()
        for j in range(1, fars):
            pass_on(o, j).wait_recv()
        keep(o, arrived.at[block_of(0, rows)]).wait()
        normed, _ = normalize(packed[span, :].astype(jnp.float32))
        scaled = (normed * r.gain_feat[...]).astype(jnp.bfloat16)
        hidden = jnp.dot(scaled, proj[...], preferred_element_type=jnp.float32)
        normed, _ = normalize(hidden)
        r.hid_ln[span, :] = (normed * r.gain_block[...]).astype(jnp.bfloat16)
        lines = r.hid_ln[span, :]
        keep_rows = r.valid[span, :]
        units = w_in.shape[1]
        tile = min(256, units)
        for c in range(units // tile):
            cols = pl.ds(c * tile, tile)
            upward = jnp.dot(lines, w_in[:, cols], preferred_element_type=jnp.float32)
            phi = 0.5 * (1.0 + lax.erf(upward * SQRT_HALF))
            slope = phi + upward * INV_SQRT_TWO_PI * jnp.exp(-0.5 * upward * upward)
            r.active[span, cols] = (keep_rows * (upward * phi)).astype(jnp.bfloat16)
            r.grad_up[span, cols] = (spare[span, cols].astype(jnp.float32) * slope).astype(
                jnp.bfloat16
            )
        r.normed_part[span, :] = contract_cols(r.grad_up[span, :], w_in[...]).astype(
            jnp.bfloat16
        )
        sum_near(s).start()

        @pl.when(o > 0)
        def _():
            pair_sum(source_of(o - 1))

    loop(parts, forward)
    pair_sum(source_of(parts - 1))
    load_conv = load(r.conv_in_hbm, spare, 4)

    pairs = [(cot, r.active, r.out_out), (r.hid_ln, r.grad_up, r.in_out)]
    made, taken = r.made, r.taken
    big = r.out_out.shape[0]

    def halve(i, k, j):
        span = block_of(owner(k), big)
        return remote(
            made.at[i, span], taken.at[i, k], r.halve_send.at[i, k], r.halve_recv.at[i, k],
            "dp", mate(j),
        )

    def make_pair(i, first, second):
        left, right, _ = pairs[i]
        a, b = owner(first), owner(second)
        both = jnp.concatenate([left[:, block_of(a, big)], left[:, block_of(b, big)]], axis=1)
        value = contract_rows(both, right[...]).astype(jnp.bfloat16)
        made[i, block_of(a, big), :] = value[:big]
        made[i, block_of(b, big), :] = value[big:]

    def make_odd(i):
        if big % 128:
            left, right, _ = pairs[i]

            def strip(t):
                made[i, block_of(t, 128), :] = contract_rows(
                    left[:, block_of(t, 128)], right[...]
                ).astype(jnp.bfloat16)

            loop(left.shape[1] // 128, strip)

        def odd(t):
            first = parts - 1 - 2 * t
            if big % 128 == 0:
                make_pair(i, first, first - half)
            halve(i, first, 0).start()
            halve(i, first - half, 0).start()

        loop(parts // 4, odd)

    def make_even(i):
        if big % 128 == 0:
            loop(parts // 4, lambda t: make_pair(i, parts - 2 - 2 * t, half - 2 - 2 * t))

    def low_bit(k):
        return (k & -k).bit_length() - 1 if k else levels

    def settle(i, k):
        j = low_bit(k)
        out = pairs[i][2]
        base = owner(k) * big
        for low in range(j):
            halve(i, k + 2**low, low).wait_recv()

        def tile(t):
            span = pl.ds(pl.multiple_of(base + t * 16, 16), 16)
            part = pl.ds(pl.multiple_of(t * 16, 16), 16)
            total = made[i, span, :].astype(jnp.float32)
            for low in range(j):
                total = total + taken[i, k + 2**low, part, :].astype(jnp.float32)
            if k:
                made[i, span, :] = total.astype(jnp.bfloat16)
            else:
                out[part, :] = total

        loop(big // 16, tile)
        if k:
            halve(i, k, j).start()

    def at_level(j):
        return [k for k in range(parts - 1, 0, -1) if low_bit(k) == j]

    make_odd(0)

    per = min(parts, max(1, 256 // share))
    channels = packed.shape[1]

    def back_chain(g):
        sources = [g * per + i for i in range(per)]
        spans = [
            pl.ds(pl.multiple_of(s * rows + piece * share, share), share) for s in sources
        ]

        def rows_of(ref):
            return jnp.concatenate([ref[span, :] for span in spans], axis=0)

        feat_norm, feat_inv = normalize(rows_of(packed).astype(jnp.float32))
        feat_ln = (feat_norm * r.gain_feat[...]).astype(jnp.bfloat16)
        hidden = jnp.dot(feat_ln, proj[...], preferred_element_type=jnp.float32)
        hid_norm, hid_inv = normalize(hidden)
        for s in sources:
            for j in range(1, fars):
                sum_far(s, j).wait_recv()
        upstream = []
        for s in sources:
            total = r.own_sum[s]
            for j in range(1, fars):
                total = total + r.far_in[s, j].astype(jnp.float32)
            upstream.append(total)
        upstream = jnp.concatenate(upstream, axis=0)
        direct = rows_of(r.valid) * rows_of(cot).astype(jnp.float32)
        grad_hidden = (
            direct + norm_back(upstream, hid_norm, hid_inv, r.gain_block[...])
        ).astype(jnp.bfloat16)
        grad_feat = contract_cols(grad_hidden, proj[...])
        grad_packed = norm_back(grad_feat, feat_norm, feat_inv, r.gain_feat[...]).astype(
            jnp.bfloat16
        )
        for i, s in enumerate(sources):
            r.grad[s] = grad_packed[i * share : (i + 1) * share]
        term = contract_rows(feat_ln, grad_hidden)
        proj_sum = r.proj_sum

        @pl.when(g == 0)
        def _():
            proj_sum[...] = term

        @pl.when(g > 0)
        def _():
            proj_sum[...] = proj_sum[...] + term

    loop(parts // per, back_chain)

    def columns(o):
        peer = lax.rem(m + o, shards)
        return remote(
            r.grad.at[:, :, block_of(peer, width)],
            r.middle.at[:, block_of(piece, share), :],
            r.col_send.at[o],
            r.col_recv.at[o],
            "mp",
            peer,
        )

    for o in range(1, shards):
        columns(o).start()
    own_columns = pltpu.make_async_copy(
        r.grad.at[:, :, block_of(m, width)],
        r.middle.at[:, block_of(piece, share), :],
        r.own_sem.at[0],
    )
    own_columns.start()
    quarter = r.proj_out.shape[1]
    r.proj_term[...] = r.proj_sum[...].astype(jnp.bfloat16)

    def proj_columns(o):
        peer = lax.rem(m + o, shards)
        return remote(
            r.proj_term.at[:, block_of(peer, quarter)],
            r.proj_in.at[o],
            r.proj_send.at[o],
            r.proj_recv.at[o],
            "mp",
            peer,
        )

    for o in range(1, shards):
        proj_columns(o).start()

    make_even(0)
    for o in range(1, shards):
        columns(o).wait_recv()
    own_columns.wait()

    def give_back(o):
        target = lax.rem(d + o, parts)
        return remote(
            r.middle.at[target],
            r.back.at[d],
            r.back_send.at[o],
            r.back_recv.at[o],
            "dp",
            target,
        )

    for o in range(1, parts):
        give_back(o).start()
    own_block = pltpu.make_async_copy(r.middle.at[d], r.back.at[d], r.own_sem.at[1])
    own_block.start()

    make_odd(1)
    for k in at_level(1):
        settle(0, k)
    make_even(1)

    for o in range(1, shards):
        proj_columns(o).wait_recv()
    small = r.proj_out.shape[0]
    proj_total = r.proj_term[:, block_of(m, quarter)].astype(jnp.float32)
    for o in range(1, shards):
        proj_total = proj_total + r.proj_in[o].astype(jnp.float32)
    r.proj_made[...] = proj_total.astype(jnp.bfloat16)

    def direct_sum(made, taken, send, recv, size):
        def copy(o):
            target = lax.rem(d + o, parts)
            return remote(
                made.at[block_of(target, size)],
                taken.at[o],
                send.at[o],
                recv.at[o],
                "dp",
                target,
            )

        return copy

    proj_copy = direct_sum(r.proj_made, r.proj_taken, r.proj_dp_send, r.proj_dp_recv, small)
    for o in range(1, parts):
        proj_copy(o).start()
    for j in range(2, levels):
        for k in at_level(j):
            settle(0, k)

    for o in range(1, parts):
        give_back(o).wait_recv()
    own_block.wait()
    load_conv.wait()
    returned = jnp.concatenate([r.back[e] for e in range(parts)], axis=0)
    strip = min(256, frames)

    def conv_strip(t):
        span = block_of(t, strip)
        frame = t * strip + lax.broadcasted_iota(jnp.int32, (strip, frames), 0)
        chosen = jnp.where(frame == r.index_row[...], 1.0, 0.0).astype(jnp.bfloat16)
        grad_features = jnp.dot(chosen, returned, preferred_element_type=jnp.float32)
        r.grad_pre[span, :] = (grad_features * gelu_slope(r.pre_act[span, :])).astype(
            jnp.bfloat16
        )

    loop(frames // strip, conv_strip)
    conv_term = contract_rows(r.grad_pre[...], spare[...])
    r.conv_made[...] = conv_term.T.astype(jnp.bfloat16)
    mini = r.conv_out.shape[0]
    conv_copy = direct_sum(r.conv_made, r.conv_taken, r.conv_dp_send, r.conv_dp_recv, mini)
    for o in range(1, parts):
        conv_copy(o).start()

    for j in range(1, levels):
        for k in at_level(j):
            settle(1, k)
    settle(0, 0)

    def finish(copy, made, taken, out, size):
        total = made[block_of(d, size), :].astype(jnp.float32)
        for o in range(1, parts):
            copy(o).wait_recv()
            total = total + taken[o].astype(jnp.float32)
        out[...] = total

    finish(proj_copy, r.proj_made, r.proj_taken, r.proj_out, small)
    finish(conv_copy, r.conv_made, r.conv_taken, r.conv_out, mini)
    settle(1, 0)

    for o in range(1, parts):
        exchange(o).wait_send()
        give_back(o).wait_send()
        proj_copy(o).wait_send()
        conv_copy(o).wait_send()

    def drain(o):
        block = arrived.at[block_of(0, rows)]
        to_near(o, block).wait_send()
        sum_near(o).wait_send()
        for j in range(1, fars):
            to_far(o, j, block).wait_send()
            pass_on(o, j).wait_send()
            sum_far(o, j).wait_send()

    loop(parts, drain)
    for o in range(1, shards):
        columns(o).wait_send()
        proj_columns(o).wait_send()
    for i in range(2):
        for k in range(1, parts):
            halve(i, k, low_bit(k)).wait_send()


def run_step(ins, vmem_ins):
    parts, shards = lax.axis_size("dp"), lax.axis_size("mp")
    frames, width = ins["outgoing"].shape
    conv_in, proj, w_in, w_out, cot = list(ins.values())[vmem_ins:]
    rows = frames // parts
    share = rows // shards
    fars = max(shards // 2, 1)
    channels, model = proj.shape
    units = w_in.shape[1]
    taps = conv_in.shape[1]
    big, small, mini, quarter = model // parts, channels // parts, taps // parts, model // shards
    bf16, f32 = jnp.bfloat16, jnp.float32
    dma = pltpu.SemaphoreType.DMA
    outs = dict(
        conv_out=jax.ShapeDtypeStruct((mini, width), f32),
        proj_out=jax.ShapeDtypeStruct((small, quarter), f32),
        in_out=jax.ShapeDtypeStruct((big, units), f32),
        out_out=jax.ShapeDtypeStruct((big, units), f32),
    )
    scratch = dict(
        w_out=pltpu.VMEM(w_out.shape, bf16),
        cot=pltpu.VMEM(cot.shape, bf16),
        proj=pltpu.VMEM(proj.shape, bf16),
        w_in=pltpu.VMEM(w_in.shape, bf16),
        spare=pltpu.VMEM((frames, max(units, taps)), bf16),
        arrived=pltpu.VMEM((frames, width), bf16),
        packed=pltpu.VMEM((frames, channels), bf16),
        hid_ln=pltpu.VMEM((frames, model), bf16),
        active=pltpu.VMEM((frames, units), bf16),
        grad_up=pltpu.VMEM((frames, units), bf16),
        normed_part=pltpu.VMEM((frames, model), bf16),
        near_in=pltpu.VMEM((parts, fars * share, model), bf16),
        staged=pltpu.VMEM((parts, fars, share, model), bf16),
        far_in=pltpu.VMEM((parts, fars, share, model), bf16),
        own_sum=pltpu.VMEM((parts, share, model), f32),
        made=pltpu.VMEM((2, model, units), bf16),
        taken=pltpu.VMEM((2, parts, big, units), bf16),
        grad=pltpu.VMEM((parts, share, channels), bf16),
        middle=pltpu.VMEM((parts, rows, width), bf16),
        back=pltpu.VMEM((parts, rows, width), bf16),
        proj_sum=pltpu.VMEM((channels, model), f32),
        proj_term=pltpu.VMEM((channels, model), bf16),
        proj_in=pltpu.VMEM((shards, channels, quarter), bf16),
        proj_made=pltpu.VMEM((channels, quarter), bf16),
        proj_taken=pltpu.VMEM((parts, small, quarter), bf16),
        grad_pre=pltpu.VMEM((frames, width), bf16),
        conv_made=pltpu.VMEM((taps, width), bf16),
        conv_taken=pltpu.VMEM((parts, mini, width), bf16),
        load_sem=dma((5,)),
        keep_sem=dma((parts,)),
        own_sem=dma((2,)),
        dp_send=dma((parts,)),
        dp_recv=dma((parts,)),
        near_send=dma((parts,)),
        near_recv=dma((parts,)),
        sum_near_send=dma((parts,)),
        sum_near_recv=dma((parts,)),
        back_send=dma((parts,)),
        back_recv=dma((parts,)),
        proj_dp_send=dma((parts,)),
        proj_dp_recv=dma((parts,)),
        conv_dp_send=dma((parts,)),
        conv_dp_recv=dma((parts,)),
        far_send=dma((parts, fars)),
        far_recv=dma((parts, fars)),
        pass_send=dma((parts, fars)),
        pass_recv=dma((parts, fars)),
        sum_far_send=dma((parts, fars)),
        sum_far_recv=dma((parts, fars)),
        col_send=dma((shards,)),
        col_recv=dma((shards,)),
        proj_send=dma((shards,)),
        proj_recv=dma((shards,)),
        halve_send=dma((2, parts)),
        halve_recv=dma((2, parts)),
    )
    names = tuple(ins) + tuple(outs) + tuple(scratch)
    vmem = pl.BlockSpec(memory_space=pltpu.VMEM)
    anywhere = pl.BlockSpec(memory_space=pl.ANY)
    return pl.pallas_call(
        functools.partial(step_kernel, parts, shards, names),
        out_shape=list(outs.values()),
        in_specs=[vmem] * vmem_ins + [anywhere] * (len(ins) - vmem_ins),
        out_specs=[vmem] * len(outs),
        scratch_shapes=list(scratch.values()),
        compiler_params=pltpu.CompilerParams(
            collective_id=1, has_side_effects=True, vmem_limit_bytes=VMEM_LIMIT
        ),
        name="step",
    )(*ins.values())


def on_device(
    conv_in,
    conv_weight,
    feature_gain,
    proj_weight,
    block_gain,
    w_in,
    w_out,
    cotangent,
    send_index,
    slot_valid,
):
    frames = conv_in.shape[0]
    pre_act = jnp.dot(conv_in, conv_weight, preferred_element_type=jnp.float32)
    features = gelu_exact(pre_act).astype(jnp.bfloat16)
    choose = (send_index[:, None] == jnp.arange(frames, dtype=send_index.dtype)).astype(jnp.bfloat16)
    outgoing = jnp.dot(choose, features, preferred_element_type=jnp.float32).astype(jnp.bfloat16)
    valid = slot_valid.astype(jnp.float32)[:, None]
    ins = dict(
        outgoing=outgoing, pre_act=pre_act, valid=valid, index_row=send_index[None, :],
        gain_feat=feature_gain[None, :], gain_block=block_gain[None, :], conv_in_hbm=conv_in,
        proj_hbm=proj_weight, w_in_hbm=w_in, w_out_hbm=w_out, cot_hbm=cotangent,
    )
    return tuple(run_step(ins, 6))


def solution(mesh):
    placed = (
        P("dp", None),
        P(None, "mp"),
        P(),
        P(),
        P(),
        P(None, "mp"),
        P(None, "mp"),
        P("dp", None),
        P("dp"),
        P("dp"),
    )
    return jax.shard_map(
        on_device,
        mesh=mesh,
        in_specs=placed,
        out_specs=(P("dp", "mp"), P("dp", "mp"), P("dp", "mp"), P("dp", "mp")),
        check_vma=False,
    )
```

```python
import functools
import types

import jax
import jax.numpy as jnp
from jax import lax
from jax.experimental import pallas as pl
from jax.experimental.pallas import tpu as pltpu
from jax.sharding import PartitionSpec as P

EPSILON = 1e-05
SQRT_HALF = 0.7071067811865476
INV_SQRT_TWO_PI = 0.3989422804014327
VMEM_LIMIT = 67043328


def gelu_exact(values):
    return 0.5 * values * (1.0 + lax.erf(values * SQRT_HALF))


def gelu_slope(values):
    return 0.5 * (1.0 + lax.erf(values * SQRT_HALF)) + values * INV_SQRT_TWO_PI * jnp.exp(
        -0.5 * values * values
    )


def normalize(values):
    row_mean = jnp.mean(values, axis=-1, keepdims=True)
    centred = values - row_mean
    inv_std = lax.rsqrt(jnp.mean(centred * centred, axis=-1, keepdims=True) + EPSILON)
    return (centred * inv_std, inv_std)


def norm_back(upstream, normed, inv_std, gain_row):
    scaled = upstream * gain_row
    first_mean = jnp.mean(scaled, axis=-1, keepdims=True)
    second_mean = jnp.mean(scaled * normed, axis=-1, keepdims=True)
    return inv_std * (scaled - first_mean - normed * second_mean)


def contract_rows(left, right):
    return lax.dot_general(
        left, right, (((0,), (0,)), ((), ())), preferred_element_type=jnp.float32
    )


def contract_cols(left, right):
    return lax.dot_general(
        left, right, (((1,), (1,)), ((), ())), preferred_element_type=jnp.float32
    )


def start_copy(src, dst, send_sem, recv_sem, axis, index):
    copy = remote(src, dst, send_sem, recv_sem, axis, index)
    copy.start()
    return copy


def remote(src, dst, send_sem, recv_sem, axis, index):
    return pltpu.make_async_remote_copy(
        src_ref=src,
        dst_ref=dst,
        send_sem=send_sem,
        recv_sem=recv_sem,
        device_id={axis: index},
        device_id_type=pl.DeviceIdType.MESH,
    )


def greet(peers):
    barrier = pltpu.get_barrier_semaphore()
    for axis, index in peers:
        pl.semaphore_signal(
            barrier, inc=1, device_id={axis: index}, device_id_type=pl.DeviceIdType.MESH
        )
    return barrier, len(peers)


def block_of(index, size):
    return pl.ds(pl.multiple_of(index * size, size), size)


def loop(count, body):
    def step(t, carry):
        body(t)
        return carry

    lax.fori_loop(0, count, step, 0)


def step_kernel(parts, shards, names, *refs):
    r = types.SimpleNamespace(**dict(zip(names, refs)))
    outgoing, arrived, packed = r.outgoing, r.arrived, r.packed
    frames, width = outgoing.shape
    rows = frames // parts
    share = rows // shards
    fars = shards // 2
    group_rows = fars * share
    levels = parts.bit_length() - 1
    half = parts // 2
    w_in, w_out, proj, cot = r.w_in, r.w_out, r.proj, r.cot
    spare = r.spare
    d = lax.axis_index("dp")
    m = lax.axis_index("mp")
    side = lax.rem(m, 2)
    line = m // 2
    near = m + 1 - 2 * side
    piece = side * fars + line

    def load(src, dst, k):
        copy = pltpu.make_async_copy(src, dst, r.load_sem.at[k])
        copy.start()
        return copy

    first_frames = r.normed_part
    strips = 4
    strip = frames // strips
    load_weight = load(r.conv_weight_hbm, r.conv_weight, 5)
    load_frames = [
        load(r.conv_in_hbm.at[block_of(t, strip)], first_frames.at[block_of(t, strip)], 6 + t)
        for t in range(strips)
    ]
    load_w_out = load(r.w_out_hbm, w_out, 0)
    load_cot = load(r.cot_hbm, cot, 1)
    load_proj = load(r.proj_hbm, proj, 2)
    load_w_in = load(r.w_in_hbm, w_in, 3)

    def flip(index, bit):
        return index + bit - 2 * bit * lax.rem(index // bit, 2)

    def owner(bits, k):
        total = 0
        for j, bit in enumerate(bits):
            total = total + bit * lax.rem(lax.rem(d // bit, 2) + lax.rem(k // 2**j, 2), 2)
        return total

    def far(j):
        return lax.rem(m + 2 * j, shards)

    peers = greet(
        [("dp", lax.rem(d + o, parts)) for o in range(1, parts)]
        + [("mp", lax.rem(m + o, shards)) for o in range(1, shards)]
    )
    r.valid[...] = jnp.broadcast_to(r.valid_row[...].astype(jnp.float32), (8, frames)).T[:, :1]

    load_weight.wait()
    weight_rows = r.conv_weight[...].T
    for t in range(strips):
        load_frames[t].wait()
        span = pl.ds(t * strip, strip)
        value = contract_cols(weight_rows, first_frames[span, :])
        r.pre_act[:, span] = value
        r.features[:, span] = gelu_exact(value).astype(jnp.bfloat16)

    def exchange(o):
        target = lax.rem(d + o, parts)
        return remote(
            outgoing.at[block_of(target, rows)],
            arrived.at[block_of(d, rows)],
            r.dp_send.at[o],
            r.dp_recv.at[o],
            "dp",
            target,
        )

    def pack(t, size):
        frame = lax.broadcasted_iota(jnp.int32, (frames, size), 0)
        chosen = jnp.where(frame == r.index_row[:, block_of(t, size)], 1.0, 0.0)
        value = jnp.dot(
            r.features[...], chosen.astype(jnp.bfloat16), preferred_element_type=jnp.float32
        )
        outgoing[block_of(t, size), :] = value.T.astype(jnp.bfloat16)

    if rows % 128 == 0:
        pl.semaphore_wait(*peers)

        def pack_and_send(t):
            pack(lax.rem(d + t + 1, parts), rows)

            @pl.when(t < parts - 1)
            def _():
                exchange(t + 1).start()

        loop(parts, pack_and_send)
    else:
        loop(frames // 128, lambda t: pack(t, 128))
        pl.semaphore_wait(*peers)
        for o in range(1, parts):
            exchange(o).start()

    def source_of(o):
        return lax.rem(d - o + parts, parts)

    def place(o):
        return packed.at[block_of(source_of(o), rows), block_of(m, width)]

    def to_far(o, j, block):
        return remote(
            block, place(o), r.far_send.at[o, j], r.far_recv.at[o, j], "mp", far(j)
        )

    def to_near(o, block):
        return remote(block, place(o), r.near_send.at[o], r.near_recv.at[o], "mp", near)

    def keep(o, block):
        return pltpu.make_async_copy(block, place(o), r.keep_sem.at[o])

    def spread(o, block):
        for j in range(1, fars):
            to_far(o, j, block).start()
        to_near(o, block).start()
        keep(o, block).start()

    def relay(o):
        exchange(o).wait_recv()
        spread(o, arrived.at[block_of(source_of(o), rows)])

    def pass_on(o, j):
        col = block_of(lax.rem(m - 2 * j + shards, shards), width)
        part = packed.at[block_of(source_of(o), rows), col]
        return remote(part, part, r.pass_send.at[o, j], r.pass_recv.at[o, j], "mp", near)

    def hand_on(o):
        for j in range(1, fars):
            to_far(o, j, arrived.at[block_of(0, rows)]).wait_recv()
            pass_on(o, j).start()

    spread(0, outgoing.at[block_of(d, rows)])

    load_w_out.wait()
    load_cot.wait()

    def grad_active(t):
        span = block_of(t, rows)
        value = jnp.dot(cot[span, :], w_out[...], preferred_element_type=jnp.float32)
        spare[span, :] = (r.valid[span, :] * value).astype(jnp.bfloat16)
        now = t // 2

        @pl.when((lax.rem(t, 2) == 1) & (t > 1))
        def _():
            relay(now)
            hand_on(now - 1)

    loop(parts, grad_active)
    load_proj.wait()
    load_w_in.wait()

    def sum_near(s):
        return remote(
            r.normed_part.at[pl.ds(s * rows + (1 - side) * group_rows, group_rows)],
            r.near_in.at[s],
            r.sum_near_send.at[s],
            r.sum_near_recv.at[s],
            "mp",
            near,
        )

    def sum_far(s, j):
        return remote(
            r.staged.at[s, j],
            r.far_in.at[s, j],
            r.sum_far_send.at[s, j],
            r.sum_far_recv.at[s, j],
            "mp",
            far(j),
        )

    def pair_sum(s):
        sum_near(s).wait_recv()
        for j in range(fars):
            at = lax.rem(line + j, fars) * share
            mine = r.normed_part[pl.ds(pl.multiple_of(s * rows + side * group_rows + at, share), share), :]
            theirs = r.near_in[s, pl.ds(pl.multiple_of(at, share), share), :]
            total = mine.astype(jnp.float32) + theirs.astype(jnp.float32)
            if j:
                r.staged[s, j] = total.astype(jnp.bfloat16)
                sum_far(s, j).start()
            else:
                r.own_sum[s] = total

    def forward(o):
        s = source_of(o)
        span = block_of(s, rows)

        @pl.when(o + half < parts)
        def _():
            relay(o + half)

        @pl.when(o + half - 1 < parts)
        def _():
            hand_on(o + half - 1)

        to_near(o, arrived.at[block_of(0, rows)]).wait_recv()
        for j in range(1, fars):
            pass_on(o, j).wait_recv()
        keep(o, arrived.at[block_of(0, rows)]).wait()
        normed, _ = normalize(packed[span, :].astype(jnp.float32))
        scaled = (normed * r.gain_feat[...]).astype(jnp.bfloat16)
        hidden = jnp.dot(scaled, proj[...], preferred_element_type=jnp.float32)
        normed, _ = normalize(hidden)
        r.hid_ln[span, :] = (normed * r.gain_block[...]).astype(jnp.bfloat16)
        lines = r.hid_ln[span, :]
        keep_rows = r.valid[span, :]
        units = w_in.shape[1]
        tile = min(256, units)
        for c in range(units // tile):
            cols = pl.ds(c * tile, tile)
            upward = jnp.dot(lines, w_in[:, cols], preferred_element_type=jnp.float32)
            phi = 0.5 * (1.0 + lax.erf(upward * SQRT_HALF))
            slope = phi + upward * INV_SQRT_TWO_PI * jnp.exp(-0.5 * upward * upward)
            r.active[span, cols] = (keep_rows * (upward * phi)).astype(jnp.bfloat16)
            r.grad_up[span, cols] = (spare[span, cols].astype(jnp.float32) * slope).astype(
                jnp.bfloat16
            )
        r.normed_part[span, :] = contract_cols(r.grad_up[span, :], w_in[...]).astype(
            jnp.bfloat16
        )
        sum_near(s).start()

        @pl.when(o > 0)
        def _():
            pair_sum(source_of(o - 1))

    loop(parts, forward)
    pair_sum(source_of(parts - 1))
    load_conv = load(r.conv_in_hbm, spare, 4)

    natural = [2**j for j in range(levels)]
    swapped = natural[1::-1] + natural[2:]
    turned = natural[1:] + natural[:1]
    big, units = r.out_out.shape
    part = units // 2

    def unit(made, taken, out, bits, send, recv):
        return types.SimpleNamespace(
            made=made, taken=taken, out=out, bits=bits, send=send, recv=recv, size=out.shape[0]
        )

    def big_unit(u, out, bits):
        return unit(
            r.made.at[u], r.taken.at[u], out.at[:, pl.ds(u % 2 * part, part)], bits,
            r.halve_send.at[u], r.halve_recv.at[u],
        )

    out_a = big_unit(0, r.out_out, natural)
    out_b = big_unit(1, r.out_out, swapped)
    in_a = big_unit(2, r.in_out, natural)
    in_b = big_unit(3, r.in_out, natural)
    sides = [(cot, r.active, 0), (cot, r.active, 1), (r.hid_ln, r.grad_up, 0), (r.hid_ln, r.grad_up, 1)]
    bigs = [out_a, out_b, in_a, in_b]
    proj_unit = unit(r.proj_made, r.proj_taken, r.proj_out, turned, r.proj_dp_send, r.proj_dp_recv)
    conv_unit = unit(r.conv_made, r.conv_taken, r.conv_out, turned, r.conv_dp_send, r.conv_dp_recv)

    def halve(x, k, j):
        return remote(
            x.made.at[block_of(owner(x.bits, k), x.size)], x.taken.at[k], x.send.at[k],
            x.recv.at[k], "dp", flip(d, x.bits[j]),
        )

    def make_pair(u, first, second):
        left, right, h = sides[u]
        x = bigs[u]
        a, b = owner(x.bits, first), owner(x.bits, second)
        both = jnp.concatenate([left[:, block_of(a, big)], left[:, block_of(b, big)]], axis=1)
        value = contract_rows(both, right[:, pl.ds(h * part, part)]).astype(jnp.bfloat16)
        x.made[block_of(a, big), :] = value[:big]
        x.made[block_of(b, big), :] = value[big:]

    def make_odd(u):
        x = bigs[u]
        if big % 128:
            left, right, h = sides[u]

            def rows_strip(t):
                x.made[block_of(t, 128), :] = contract_rows(
                    left[:, block_of(t, 128)], right[:, pl.ds(h * part, part)]
                ).astype(jnp.bfloat16)

            loop(left.shape[1] // 128, rows_strip)

        def odd(t):
            first = parts - 1 - 2 * t
            if big % 128 == 0:
                make_pair(u, first, first - half)
            halve(x, first, 0).start()
            halve(x, first - half, 0).start()

        loop(parts // 4, odd)

    def make_even(u):
        if big % 128 == 0:
            loop(parts // 4, lambda t: make_pair(u, parts - 2 - 2 * t, half - 2 - 2 * t))

    def low_bit(k):
        return (k & -k).bit_length() - 1 if k else levels

    def settle(x, k):
        j = low_bit(k)
        base = owner(x.bits, k) * x.size
        for low in range(j):
            halve(x, k + 2**low, low).wait_recv()

        def tile(t):
            span = pl.ds(pl.multiple_of(base + t * 16, 16), 16)
            rows_in = pl.ds(pl.multiple_of(t * 16, 16), 16)
            total = x.made[span, :].astype(jnp.float32)
            for low in range(j):
                total = total + x.taken[k + 2**low, rows_in, :].astype(jnp.float32)
            if k:
                x.made[span, :] = total.astype(jnp.bfloat16)
            else:
                x.out[rows_in, :] = total

        loop(x.size // 16, tile)
        if k:
            halve(x, k, j).start()

    def settle_level(x, j):
        for k in range(parts - 1, 0, -1):
            if low_bit(k) == j:
                settle(x, k)

    def send_first(x):
        for k in range(parts - 1, 0, -2):
            halve(x, k, 0).start()

    make_odd(0)
    make_odd(1)
    make_odd(2)

    per = min(parts, max(1, 256 // share))
    channels = packed.shape[1]

    def back_chain(g):
        sources = [g * per + i for i in range(per)]
        spans = [
            pl.ds(pl.multiple_of(s * rows + piece * share, share), share) for s in sources
        ]

        def rows_of(ref):
            return jnp.concatenate([ref[span, :] for span in spans], axis=0)

        feat_norm, feat_inv = normalize(rows_of(packed).astype(jnp.float32))
        feat_ln = (feat_norm * r.gain_feat[...]).astype(jnp.bfloat16)
        hidden = jnp.dot(feat_ln, proj[...], preferred_element_type=jnp.float32)
        hid_norm, hid_inv = normalize(hidden)
        for s in sources:
            for j in range(1, fars):
                sum_far(s, j).wait_recv()
        upstream = []
        for s in sources:
            total = r.own_sum[s]
            for j in range(1, fars):
                total = total + r.far_in[s, j].astype(jnp.float32)
            upstream.append(total)
        upstream = jnp.concatenate(upstream, axis=0)
        direct = rows_of(r.valid) * rows_of(cot).astype(jnp.float32)
        grad_hidden = (
            direct + norm_back(upstream, hid_norm, hid_inv, r.gain_block[...])
        ).astype(jnp.bfloat16)
        grad_feat = contract_cols(grad_hidden, proj[...])
        grad_packed = norm_back(grad_feat, feat_norm, feat_inv, r.gain_feat[...]).astype(
            jnp.bfloat16
        )
        for i, s in enumerate(sources):
            r.grad[s] = grad_packed[i * share : (i + 1) * share]
        term = contract_rows(feat_ln, grad_hidden)
        proj_sum = r.proj_sum

        @pl.when(g == 0)
        def _():
            proj_sum[...] = term

        @pl.when(g > 0)
        def _():
            proj_sum[...] = proj_sum[...] + term

    loop(parts // per, back_chain)

    def columns(o):
        peer = lax.rem(m + o, shards)
        return remote(
            r.grad.at[:, :, block_of(peer, width)],
            r.middle.at[:, block_of(piece, share), :],
            r.col_send.at[o],
            r.col_recv.at[o],
            "mp",
            peer,
        )

    for o in range(1, shards):
        columns(o).start()
    own_columns = pltpu.make_async_copy(
        r.grad.at[:, :, block_of(m, width)],
        r.middle.at[:, block_of(piece, share), :],
        r.own_sem.at[0],
    )
    own_columns.start()
    quarter = r.proj_out.shape[1]
    r.proj_term[...] = r.proj_sum[...].astype(jnp.bfloat16)

    def proj_columns(o):
        peer = lax.rem(m + o, shards)
        return remote(
            r.proj_term.at[:, block_of(peer, quarter)],
            r.proj_in.at[o],
            r.proj_send.at[o],
            r.proj_recv.at[o],
            "mp",
            peer,
        )

    for o in range(1, shards):
        proj_columns(o).start()

    make_even(0)
    make_even(1)
    for o in range(1, shards):
        columns(o).wait_recv()
    own_columns.wait()

    def give_back(o):
        target = lax.rem(d + o, parts)
        return remote(
            r.middle.at[target],
            r.back.at[d],
            r.back_send.at[o],
            r.back_recv.at[o],
            "dp",
            target,
        )

    for o in range(1, parts):
        give_back(o).start()
    own_block = pltpu.make_async_copy(r.middle.at[d], r.back.at[d], r.own_sem.at[1])
    own_block.start()

    settle_level(out_a, 1)
    settle_level(out_b, 1)
    make_odd(3)
    make_even(2)
    make_even(3)

    for o in range(1, shards):
        proj_columns(o).wait_recv()
    proj_total = r.proj_term[:, block_of(m, quarter)].astype(jnp.float32)
    for o in range(1, shards):
        proj_total = proj_total + r.proj_in[o].astype(jnp.float32)
    r.proj_made[...] = proj_total.astype(jnp.bfloat16)

    send_first(proj_unit)
    for j in range(2, levels):
        settle_level(out_a, j)
        settle_level(out_b, j)

    for o in range(1, parts):
        give_back(o).wait_recv()
    own_block.wait()
    load_conv.wait()
    returned = jnp.concatenate([r.back[e] for e in range(parts)], axis=0).T
    tile = min(256, frames)

    def conv_back(t):
        span = block_of(t, tile)
        frame = t * tile + lax.broadcasted_iota(jnp.int32, (tile, frames), 0)
        chosen = jnp.where(frame == r.index_row[...], 1.0, 0.0).astype(jnp.bfloat16)
        grad_features = contract_cols(returned, chosen)
        r.grad_pre[:, span] = (grad_features * gelu_slope(r.pre_act[:, span])).astype(jnp.bfloat16)

    loop(frames // tile, conv_back)
    conv_term = jnp.dot(r.grad_pre[...], spare[...], preferred_element_type=jnp.float32)
    r.conv_made[...] = conv_term.T.astype(jnp.bfloat16)
    send_first(conv_unit)

    settle_level(proj_unit, 1)
    settle_level(in_a, 1)
    settle_level(conv_unit, 1)
    settle(out_a, 0)
    settle(out_b, 0)
    for j in range(2, levels):
        settle_level(proj_unit, j)
        settle_level(conv_unit, j)
    settle_level(in_b, 1)
    for j in range(2, levels):
        settle_level(in_a, j)
        settle_level(in_b, j)
    settle(proj_unit, 0)
    settle(conv_unit, 0)
    settle(in_a, 0)
    settle(in_b, 0)

    for o in range(1, parts):
        exchange(o).wait_send()
        give_back(o).wait_send()

    def drain(o):
        block = arrived.at[block_of(0, rows)]
        to_near(o, block).wait_send()
        sum_near(o).wait_send()
        for j in range(1, fars):
            to_far(o, j, block).wait_send()
            pass_on(o, j).wait_send()
            sum_far(o, j).wait_send()

    loop(parts, drain)
    for o in range(1, shards):
        columns(o).wait_send()
        proj_columns(o).wait_send()
    for x in bigs + [proj_unit, conv_unit]:
        for k in range(1, parts):
            halve(x, k, low_bit(k)).wait_send()


def run_step(ins, vmem_ins):
    parts, shards = lax.axis_size("dp"), lax.axis_size("mp")
    conv_in, conv_weight, proj, w_in, w_out, cot = list(ins.values())[vmem_ins:]
    frames, width = conv_in.shape[0], conv_weight.shape[1]
    rows = frames // parts
    share = rows // shards
    fars = max(shards // 2, 1)
    channels, model = proj.shape
    units = w_in.shape[1]
    taps = conv_in.shape[1]
    big, small, mini, quarter = model // parts, channels // parts, taps // parts, model // shards
    bf16, f32 = jnp.bfloat16, jnp.float32
    dma = pltpu.SemaphoreType.DMA
    outs = dict(
        conv_out=jax.ShapeDtypeStruct((mini, width), f32),
        proj_out=jax.ShapeDtypeStruct((small, quarter), f32),
        in_out=jax.ShapeDtypeStruct((big, units), f32),
        out_out=jax.ShapeDtypeStruct((big, units), f32),
    )
    scratch = dict(
        w_out=pltpu.VMEM(w_out.shape, bf16),
        cot=pltpu.VMEM(cot.shape, bf16),
        proj=pltpu.VMEM(proj.shape, bf16),
        w_in=pltpu.VMEM(w_in.shape, bf16),
        spare=pltpu.VMEM((frames, max(units, taps)), bf16),
        conv_weight=pltpu.VMEM(conv_weight.shape, bf16),
        valid=pltpu.VMEM((frames, 1), f32),
        pre_act=pltpu.VMEM((width, frames), f32),
        features=pltpu.VMEM((width, frames), bf16),
        outgoing=pltpu.VMEM((frames, width), bf16),
        arrived=pltpu.VMEM((frames, width), bf16),
        packed=pltpu.VMEM((frames, channels), bf16),
        hid_ln=pltpu.VMEM((frames, model), bf16),
        active=pltpu.VMEM((frames, units), bf16),
        grad_up=pltpu.VMEM((frames, units), bf16),
        normed_part=pltpu.VMEM((frames, model), bf16),
        near_in=pltpu.VMEM((parts, fars * share, model), bf16),
        staged=pltpu.VMEM((parts, fars, share, model), bf16),
        far_in=pltpu.VMEM((parts, fars, share, model), bf16),
        own_sum=pltpu.VMEM((parts, share, model), f32),
        made=pltpu.VMEM((4, model, units // 2), bf16),
        taken=pltpu.VMEM((4, parts, big, units // 2), bf16),
        grad=pltpu.VMEM((parts, share, channels), bf16),
        middle=pltpu.VMEM((parts, rows, width), bf16),
        back=pltpu.VMEM((parts, rows, width), bf16),
        proj_sum=pltpu.VMEM((channels, model), f32),
        proj_term=pltpu.VMEM((channels, model), bf16),
        proj_in=pltpu.VMEM((shards, channels, quarter), bf16),
        proj_made=pltpu.VMEM((channels, quarter), bf16),
        proj_taken=pltpu.VMEM((parts, small, quarter), bf16),
        grad_pre=pltpu.VMEM((width, frames), bf16),
        conv_made=pltpu.VMEM((taps, width), bf16),
        conv_taken=pltpu.VMEM((parts, mini, width), bf16),
        load_sem=dma((10,)),
        keep_sem=dma((parts,)),
        own_sem=dma((2,)),
        dp_send=dma((parts,)),
        dp_recv=dma((parts,)),
        near_send=dma((parts,)),
        near_recv=dma((parts,)),
        sum_near_send=dma((parts,)),
        sum_near_recv=dma((parts,)),
        back_send=dma((parts,)),
        back_recv=dma((parts,)),
        proj_dp_send=dma((parts,)),
        proj_dp_recv=dma((parts,)),
        conv_dp_send=dma((parts,)),
        conv_dp_recv=dma((parts,)),
        far_send=dma((parts, fars)),
        far_recv=dma((parts, fars)),
        pass_send=dma((parts, fars)),
        pass_recv=dma((parts, fars)),
        sum_far_send=dma((parts, fars)),
        sum_far_recv=dma((parts, fars)),
        col_send=dma((shards,)),
        col_recv=dma((shards,)),
        proj_send=dma((shards,)),
        proj_recv=dma((shards,)),
        halve_send=dma((4, parts)),
        halve_recv=dma((4, parts)),
    )
    names = tuple(ins) + tuple(outs) + tuple(scratch)
    vmem = pl.BlockSpec(memory_space=pltpu.VMEM)
    anywhere = pl.BlockSpec(memory_space=pl.ANY)
    return pl.pallas_call(
        functools.partial(step_kernel, parts, shards, names),
        out_shape=list(outs.values()),
        in_specs=[vmem] * vmem_ins + [anywhere] * (len(ins) - vmem_ins),
        out_specs=[vmem] * len(outs),
        scratch_shapes=list(scratch.values()),
        compiler_params=pltpu.CompilerParams(
            collective_id=1, has_side_effects=True, vmem_limit_bytes=VMEM_LIMIT
        ),
        name="step",
    )(*ins.values())


def hand_over_kernel(count, *refs):
    for i in range(count):
        refs[count + i][...] = refs[i][...]


def hand_over(results):
    return pl.pallas_call(
        functools.partial(hand_over_kernel, len(results)),
        out_shape=[jax.ShapeDtypeStruct(value.shape, value.dtype) for value in results],
        name="hand_over",
    )(*results)


def on_device(
    conv_in,
    conv_weight,
    feature_gain,
    proj_weight,
    block_gain,
    w_in,
    w_out,
    cotangent,
    send_index,
    slot_valid,
):
    ins = dict(
        valid_row=slot_valid[None, :], index_row=send_index[None, :],
        gain_feat=feature_gain[None, :], gain_block=block_gain[None, :], conv_in_hbm=conv_in,
        conv_weight_hbm=conv_weight, proj_hbm=proj_weight, w_in_hbm=w_in, w_out_hbm=w_out,
        cot_hbm=cotangent,
    )
    return tuple(hand_over(run_step(ins, 4)))


def solution(mesh):
    placed = (
        P("dp", None),
        P(None, "mp"),
        P(),
        P(),
        P(),
        P(None, "mp"),
        P(None, "mp"),
        P("dp", None),
        P("dp"),
        P("dp"),
    )
    return jax.shard_map(
        on_device,
        mesh=mesh,
        in_specs=placed,
        out_specs=(P("dp", "mp"), P("dp", "mp"), P("dp", "mp"), P("dp", "mp")),
        check_vma=False,
    )
```

```python
import functools
import types

import jax
import jax.numpy as jnp
from jax import lax
from jax.experimental import pallas as pl
from jax.experimental.pallas import tpu as pltpu
from jax.sharding import PartitionSpec as P

EPSILON = 1e-05
SQRT_HALF = 0.7071067811865476
INV_SQRT_TWO_PI = 0.3989422804014327
VMEM_LIMIT = 67043328


def gelu_exact(values):
    return 0.5 * values * (1.0 + lax.erf(values * SQRT_HALF))


def gelu_slope(values):
    return 0.5 * (1.0 + lax.erf(values * SQRT_HALF)) + values * INV_SQRT_TWO_PI * jnp.exp(
        -0.5 * values * values
    )


def normalize(values):
    row_mean = jnp.mean(values, axis=-1, keepdims=True)
    centred = values - row_mean
    inv_std = lax.rsqrt(jnp.mean(centred * centred, axis=-1, keepdims=True) + EPSILON)
    return (centred * inv_std, inv_std)


def norm_back(upstream, normed, inv_std, gain_row):
    scaled = upstream * gain_row
    first_mean = jnp.mean(scaled, axis=-1, keepdims=True)
    second_mean = jnp.mean(scaled * normed, axis=-1, keepdims=True)
    return inv_std * (scaled - first_mean - normed * second_mean)


def contract_rows(left, right):
    return lax.dot_general(
        left, right, (((0,), (0,)), ((), ())), preferred_element_type=jnp.float32
    )


def contract_cols(left, right):
    return lax.dot_general(
        left, right, (((1,), (1,)), ((), ())), preferred_element_type=jnp.float32
    )


def start_copy(src, dst, send_sem, recv_sem, axis, index):
    copy = remote(src, dst, send_sem, recv_sem, axis, index)
    copy.start()
    return copy


def remote(src, dst, send_sem, recv_sem, axis, index):
    return pltpu.make_async_remote_copy(
        src_ref=src,
        dst_ref=dst,
        send_sem=send_sem,
        recv_sem=recv_sem,
        device_id={axis: index},
        device_id_type=pl.DeviceIdType.MESH,
    )


def greet(peers):
    barrier = pltpu.get_barrier_semaphore()
    for axis, index in peers:
        pl.semaphore_signal(
            barrier, inc=1, device_id={axis: index}, device_id_type=pl.DeviceIdType.MESH
        )
    return barrier, len(peers)


def block_of(index, size):
    return pl.ds(pl.multiple_of(index * size, size), size)


def loop(count, body):
    def step(t, carry):
        body(t)
        return carry

    lax.fori_loop(0, count, step, 0)


def step_kernel(parts, shards, names, *refs):
    r = types.SimpleNamespace(**dict(zip(names, refs)))
    outgoing, arrived, packed = r.outgoing, r.arrived, r.packed
    frames, width = outgoing.shape
    rows = frames // parts
    share = rows // shards
    fars = shards // 2
    group_rows = fars * share
    levels = parts.bit_length() - 1
    half = parts // 2
    w_in, w_out, proj, cot = r.w_in, r.w_out, r.proj, r.cot
    spare = r.spare
    d = lax.axis_index("dp")
    m = lax.axis_index("mp")
    side = lax.rem(m, 2)
    line = m // 2
    near = m + 1 - 2 * side
    piece = side * fars + line

    def load(src, dst, k):
        copy = pltpu.make_async_copy(src, dst, r.load_sem.at[k])
        copy.start()
        return copy

    first_frames = r.normed_part
    strips = 4
    strip = frames // strips
    load_weight = load(r.conv_weight_hbm, r.conv_weight, 5)
    load_frames = [
        load(r.conv_in_hbm.at[block_of(t, strip)], first_frames.at[block_of(t, strip)], 6 + t)
        for t in range(strips)
    ]
    load_w_out = load(r.w_out_hbm, w_out, 0)
    load_cot = load(r.cot_hbm, cot, 1)
    load_proj = load(r.proj_hbm, proj, 2)
    load_w_in = load(r.w_in_hbm, w_in, 3)

    def flip(index, bit):
        return index + bit - 2 * bit * lax.rem(index // bit, 2)

    def owner(bits, k):
        total = 0
        for j, bit in enumerate(bits):
            total = total + bit * lax.rem(lax.rem(d // bit, 2) + lax.rem(k // 2**j, 2), 2)
        return total

    def far(j):
        return lax.rem(m + 2 * j, shards)

    peers = greet(
        [("dp", lax.rem(d + o, parts)) for o in range(1, parts)]
        + [("mp", lax.rem(m + o, shards)) for o in range(1, shards)]
    )
    r.valid[...] = jnp.broadcast_to(r.valid_row[...].astype(jnp.float32), (8, frames)).T[:, :1]

    load_weight.wait()
    weight_rows = r.conv_weight[...].T
    for t in range(strips):
        load_frames[t].wait()
        span = pl.ds(t * strip, strip)
        value = contract_cols(weight_rows, first_frames[span, :])
        r.pre_act[:, span] = value
        r.features[:, span] = gelu_exact(value).astype(jnp.bfloat16)

    def exchange(o):
        target = lax.rem(d + o, parts)
        return remote(
            outgoing.at[block_of(target, rows)],
            arrived.at[block_of(d, rows)],
            r.dp_send.at[o],
            r.dp_recv.at[o],
            "dp",
            target,
        )

    def pack(t, size):
        frame = lax.broadcasted_iota(jnp.int32, (frames, size), 0)
        chosen = jnp.where(frame == r.index_row[:, block_of(t, size)], 1.0, 0.0)
        value = jnp.dot(
            r.features[...], chosen.astype(jnp.bfloat16), preferred_element_type=jnp.float32
        )
        outgoing[block_of(t, size), :] = value.T.astype(jnp.bfloat16)

    if rows % 128 == 0:
        pl.semaphore_wait(*peers)

        def pack_and_send(t):
            pack(lax.rem(d + t + 1, parts), rows)

            @pl.when(t < parts - 1)
            def _():
                exchange(t + 1).start()

        loop(parts, pack_and_send)
    else:
        loop(frames // 128, lambda t: pack(t, 128))
        pl.semaphore_wait(*peers)
        for o in range(1, parts):
            exchange(o).start()

    def source_of(o):
        return lax.rem(d - o + parts, parts)

    def place(o):
        return packed.at[block_of(source_of(o), rows), block_of(m, width)]

    def to_far(o, j, block):
        return remote(
            block, place(o), r.far_send.at[o, j], r.far_recv.at[o, j], "mp", far(j)
        )

    def to_near(o, block):
        return remote(block, place(o), r.near_send.at[o], r.near_recv.at[o], "mp", near)

    def keep(o, block):
        return pltpu.make_async_copy(block, place(o), r.keep_sem.at[o])

    def spread(o, block):
        for j in range(1, fars):
            to_far(o, j, block).start()
        to_near(o, block).start()
        keep(o, block).start()

    def relay(o):
        exchange(o).wait_recv()
        spread(o, arrived.at[block_of(source_of(o), rows)])

    def pass_on(o, j):
        col = block_of(lax.rem(m - 2 * j + shards, shards), width)
        part = packed.at[block_of(source_of(o), rows), col]
        return remote(part, part, r.pass_send.at[o, j], r.pass_recv.at[o, j], "mp", near)

    def hand_on(o):
        for j in range(1, fars):
            to_far(o, j, arrived.at[block_of(0, rows)]).wait_recv()
            pass_on(o, j).start()

    spread(0, outgoing.at[block_of(d, rows)])

    load_w_out.wait()
    load_cot.wait()

    def grad_active(t):
        span = block_of(t, rows)
        value = jnp.dot(cot[span, :], w_out[...], preferred_element_type=jnp.float32)
        spare[span, :] = (r.valid[span, :] * value).astype(jnp.bfloat16)
        now = t // 2

        @pl.when((lax.rem(t, 2) == 1) & (t > 1))
        def _():
            relay(now)
            hand_on(now - 1)

    loop(parts, grad_active)
    load_proj.wait()
    load_w_in.wait()

    def sum_near(s):
        return remote(
            r.normed_part.at[pl.ds(s * rows + (1 - side) * group_rows, group_rows)],
            r.near_in.at[s],
            r.sum_near_send.at[s],
            r.sum_near_recv.at[s],
            "mp",
            near,
        )

    def sum_far(s, j):
        return remote(
            r.staged.at[s, j],
            r.far_in.at[s, j],
            r.sum_far_send.at[s, j],
            r.sum_far_recv.at[s, j],
            "mp",
            far(j),
        )

    def pair_sum(s):
        sum_near(s).wait_recv()
        for j in range(fars):
            at = lax.rem(line + j, fars) * share
            mine = r.normed_part[pl.ds(pl.multiple_of(s * rows + side * group_rows + at, share), share), :]
            theirs = r.near_in[s, pl.ds(pl.multiple_of(at, share), share), :]
            total = mine.astype(jnp.float32) + theirs.astype(jnp.float32)
            if j:
                r.staged[s, j] = total.astype(jnp.bfloat16)
                sum_far(s, j).start()
            else:
                r.own_sum[s] = total

    def forward(o):
        s = source_of(o)
        span = block_of(s, rows)

        @pl.when(o + half < parts)
        def _():
            relay(o + half)

        @pl.when(o + half - 1 < parts)
        def _():
            hand_on(o + half - 1)

        to_near(o, arrived.at[block_of(0, rows)]).wait_recv()
        for j in range(1, fars):
            pass_on(o, j).wait_recv()
        keep(o, arrived.at[block_of(0, rows)]).wait()
        normed, _ = normalize(packed[span, :].astype(jnp.float32))
        scaled = (normed * r.gain_feat[...]).astype(jnp.bfloat16)
        hidden = jnp.dot(scaled, proj[...], preferred_element_type=jnp.float32)
        normed, _ = normalize(hidden)
        r.hid_ln[span, :] = (normed * r.gain_block[...]).astype(jnp.bfloat16)
        lines = r.hid_ln[span, :]
        keep_rows = r.valid[span, :]
        units = w_in.shape[1]
        tile = min(256, units)
        for c in range(units // tile):
            cols = pl.ds(c * tile, tile)
            upward = jnp.dot(lines, w_in[:, cols], preferred_element_type=jnp.float32)
            phi = 0.5 * (1.0 + lax.erf(upward * SQRT_HALF))
            slope = phi + upward * INV_SQRT_TWO_PI * jnp.exp(-0.5 * upward * upward)
            r.active[span, cols] = (keep_rows * (upward * phi)).astype(jnp.bfloat16)
            r.grad_up[span, cols] = (spare[span, cols].astype(jnp.float32) * slope).astype(
                jnp.bfloat16
            )
        r.normed_part[span, :] = contract_cols(r.grad_up[span, :], w_in[...]).astype(
            jnp.bfloat16
        )
        sum_near(s).start()

        @pl.when(o > 0)
        def _():
            pair_sum(source_of(o - 1))

    loop(parts, forward)
    pair_sum(source_of(parts - 1))
    load_conv = load(r.conv_in_hbm, spare, 4)

    natural = [2**j for j in range(levels)]
    swapped = natural[1::-1] + natural[2:]
    big, units = r.out_out.shape
    part = units // 2

    def unit(made, taken, out, bits, send, recv):
        return types.SimpleNamespace(
            made=made, taken=taken, out=out, bits=bits, send=send, recv=recv, size=out.shape[0]
        )

    def big_unit(u, out, bits):
        return unit(
            r.made.at[u], r.taken.at[u], out.at[:, pl.ds(u % 2 * part, part)], bits,
            r.halve_send.at[u], r.halve_recv.at[u],
        )

    out_a = big_unit(0, r.out_out, natural)
    out_b = big_unit(1, r.out_out, swapped)
    in_a = big_unit(2, r.in_out, natural)
    in_b = big_unit(3, r.in_out, natural)
    sides = [(cot, r.active, 0), (cot, r.active, 1), (r.hid_ln, r.grad_up, 0), (r.hid_ln, r.grad_up, 1)]
    bigs = [out_a, out_b, in_a, in_b]
    proj_unit = unit(r.proj_made, r.proj_taken, r.proj_out, natural, r.proj_dp_send, r.proj_dp_recv)
    conv_unit = unit(r.conv_made, r.conv_taken, r.conv_out, natural, r.conv_dp_send, r.conv_dp_recv)

    def halve(x, k, j):
        return remote(
            x.made.at[block_of(owner(x.bits, k), x.size)], x.taken.at[k], x.send.at[k],
            x.recv.at[k], "dp", flip(d, x.bits[j]),
        )

    def make_pair(u, first, second):
        left, right, h = sides[u]
        x = bigs[u]
        a, b = owner(x.bits, first), owner(x.bits, second)
        both = jnp.concatenate([left[:, block_of(a, big)], left[:, block_of(b, big)]], axis=1)
        value = contract_rows(both, right[:, pl.ds(h * part, part)]).astype(jnp.bfloat16)
        x.made[block_of(a, big), :] = value[:big]
        x.made[block_of(b, big), :] = value[big:]

    def make_odd(u, sent):
        x = bigs[u]
        if big % 128:
            left, right, h = sides[u]

            def rows_strip(t):
                x.made[block_of(t, 128), :] = contract_rows(
                    left[:, block_of(t, 128)], right[:, pl.ds(h * part, part)]
                ).astype(jnp.bfloat16)

            loop(left.shape[1] // 128, rows_strip)

        def odd(t):
            first = parts - 1 - 2 * t
            if big % 128 == 0:
                make_pair(u, first, first - half)
            if sent:
                send_pair(x, t)

        loop(parts // 4, odd)

    def send_pair(x, t):
        first = parts - 1 - 2 * t
        halve(x, first, 0).start()
        halve(x, first - half, 0).start()

    def send_pairs(x, start, stop):
        for t in range(start, stop):
            send_pair(x, t)

    def make_even(u):
        if big % 128 == 0:
            loop(parts // 4, lambda t: make_pair(u, parts - 2 - 2 * t, half - 2 - 2 * t))

    def low_bit(k):
        return (k & -k).bit_length() - 1 if k else levels

    def settle(x, k):
        j = low_bit(k)
        base = owner(x.bits, k) * x.size
        for low in range(j):
            halve(x, k + 2**low, low).wait_recv()

        def tile(t):
            span = pl.ds(pl.multiple_of(base + t * 16, 16), 16)
            rows_in = pl.ds(pl.multiple_of(t * 16, 16), 16)
            total = x.made[span, :].astype(jnp.float32)
            for low in range(j):
                total = total + x.taken[k + 2**low, rows_in, :].astype(jnp.float32)
            if k:
                x.made[span, :] = total.astype(jnp.bfloat16)
            else:
                x.out[rows_in, :] = total

        loop(x.size // 16, tile)
        if k:
            halve(x, k, j).start()

    def settle_level(x, j):
        for k in range(parts - 1, 0, -1):
            if low_bit(k) == j:
                settle(x, k)

    def send_first(x):
        for k in range(parts - 1, 0, -2):
            halve(x, k, 0).start()

    quarter_way = max(1, parts // 8)
    make_odd(0, True)
    make_odd(1, True)
    make_odd(2, False)
    send_pairs(in_a, 0, quarter_way)

    per = min(parts, max(1, 256 // share))
    channels = packed.shape[1]

    def back_chain(g):
        sources = [g * per + i for i in range(per)]
        spans = [
            pl.ds(pl.multiple_of(s * rows + piece * share, share), share) for s in sources
        ]

        def rows_of(ref):
            return jnp.concatenate([ref[span, :] for span in spans], axis=0)

        feat_norm, feat_inv = normalize(rows_of(packed).astype(jnp.float32))
        feat_ln = (feat_norm * r.gain_feat[...]).astype(jnp.bfloat16)
        hidden = jnp.dot(feat_ln, proj[...], preferred_element_type=jnp.float32)
        hid_norm, hid_inv = normalize(hidden)
        for s in sources:
            for j in range(1, fars):
                sum_far(s, j).wait_recv()
        upstream = []
        for s in sources:
            total = r.own_sum[s]
            for j in range(1, fars):
                total = total + r.far_in[s, j].astype(jnp.float32)
            upstream.append(total)
        upstream = jnp.concatenate(upstream, axis=0)
        direct = rows_of(r.valid) * rows_of(cot).astype(jnp.float32)
        grad_hidden = (
            direct + norm_back(upstream, hid_norm, hid_inv, r.gain_block[...])
        ).astype(jnp.bfloat16)
        grad_feat = contract_cols(grad_hidden, proj[...])
        grad_packed = norm_back(grad_feat, feat_norm, feat_inv, r.gain_feat[...]).astype(
            jnp.bfloat16
        )
        for i, s in enumerate(sources):
            r.grad[s] = grad_packed[i * share : (i + 1) * share]
        term = contract_rows(feat_ln, grad_hidden)
        proj_sum = r.proj_sum

        @pl.when(g == 0)
        def _():
            proj_sum[...] = term

        @pl.when(g > 0)
        def _():
            proj_sum[...] = proj_sum[...] + term

    loop(parts // per, back_chain)

    def columns(o):
        peer = lax.rem(m + o, shards)
        return remote(
            r.grad.at[:, :, block_of(peer, width)],
            r.middle.at[:, block_of(piece, share), :],
            r.col_send.at[o],
            r.col_recv.at[o],
            "mp",
            peer,
        )

    for o in range(1, shards):
        columns(o).start()
    own_columns = pltpu.make_async_copy(
        r.grad.at[:, :, block_of(m, width)],
        r.middle.at[:, block_of(piece, share), :],
        r.own_sem.at[0],
    )
    own_columns.start()
    quarter = r.proj_out.shape[1]
    r.proj_term[...] = r.proj_sum[...].astype(jnp.bfloat16)

    def proj_columns(o):
        peer = lax.rem(m + o, shards)
        return remote(
            r.proj_term.at[:, block_of(peer, quarter)],
            r.proj_in.at[o],
            r.proj_send.at[o],
            r.proj_recv.at[o],
            "mp",
            peer,
        )

    for o in range(1, shards):
        proj_columns(o).start()

    make_even(0)
    settle_level(out_a, 1)
    make_even(1)
    make_odd(3, False)
    make_even(2)
    make_even(3)
    for o in range(1, shards):
        columns(o).wait_recv()
    own_columns.wait()

    def give_back(o):
        target = lax.rem(d + o, parts)
        return remote(
            r.middle.at[target],
            r.back.at[d],
            r.back_send.at[o],
            r.back_recv.at[o],
            "dp",
            target,
        )

    for o in range(1, parts):
        give_back(o).start()
    own_block = pltpu.make_async_copy(r.middle.at[d], r.back.at[d], r.own_sem.at[1])
    own_block.start()

    settle_level(out_b, 1)
    send_pairs(in_a, quarter_way, parts // 4)
    send_pairs(in_b, 0, quarter_way)
    for j in range(2, levels):
        settle_level(out_a, j)
    settle_level(in_a, 1)

    for o in range(1, shards):
        proj_columns(o).wait_recv()
    proj_total = r.proj_term[:, block_of(m, quarter)].astype(jnp.float32)
    for o in range(1, shards):
        proj_total = proj_total + r.proj_in[o].astype(jnp.float32)
    r.proj_made[...] = proj_total.astype(jnp.bfloat16)

    send_first(proj_unit)

    for o in range(1, parts):
        give_back(o).wait_recv()
    own_block.wait()
    load_conv.wait()
    for j in range(2, levels):
        settle_level(out_b, j)
    returned = jnp.concatenate([r.back[e] for e in range(parts)], axis=0).T
    tile = min(256, frames)

    def conv_back(t):
        span = block_of(t, tile)
        frame = t * tile + lax.broadcasted_iota(jnp.int32, (tile, frames), 0)
        chosen = jnp.where(frame == r.index_row[...], 1.0, 0.0).astype(jnp.bfloat16)
        grad_features = contract_cols(returned, chosen)
        r.grad_pre[:, span] = (grad_features * gelu_slope(r.pre_act[:, span])).astype(jnp.bfloat16)

    loop(frames // tile, conv_back)
    conv_term = jnp.dot(r.grad_pre[...], spare[...], preferred_element_type=jnp.float32)
    r.conv_made[...] = conv_term.T.astype(jnp.bfloat16)
    send_first(conv_unit)
    send_pairs(in_b, quarter_way, parts // 4)

    for j in range(2, levels):
        settle_level(in_a, j)
    settle_level(proj_unit, 1)
    settle_level(in_b, 1)
    settle_level(conv_unit, 1)
    settle(out_a, 0)
    settle(out_b, 0)
    for j in range(2, levels):
        settle_level(in_b, j)
        settle_level(proj_unit, j)
        settle_level(conv_unit, j)
    settle(in_a, 0)
    settle(proj_unit, 0)
    settle(conv_unit, 0)
    settle(in_b, 0)

    for o in range(1, parts):
        exchange(o).wait_send()
        give_back(o).wait_send()

    def drain(o):
        block = arrived.at[block_of(0, rows)]
        to_near(o, block).wait_send()
        sum_near(o).wait_send()
        for j in range(1, fars):
            to_far(o, j, block).wait_send()
            pass_on(o, j).wait_send()
            sum_far(o, j).wait_send()

    loop(parts, drain)
    for o in range(1, shards):
        columns(o).wait_send()
        proj_columns(o).wait_send()
    for x in bigs + [proj_unit, conv_unit]:
        for k in range(1, parts):
            halve(x, k, low_bit(k)).wait_send()


def run_step(ins, vmem_ins):
    parts, shards = lax.axis_size("dp"), lax.axis_size("mp")
    conv_in, conv_weight, proj, w_in, w_out, cot = list(ins.values())[vmem_ins:]
    frames, width = conv_in.shape[0], conv_weight.shape[1]
    rows = frames // parts
    share = rows // shards
    fars = max(shards // 2, 1)
    channels, model = proj.shape
    units = w_in.shape[1]
    taps = conv_in.shape[1]
    big, small, mini, quarter = model // parts, channels // parts, taps // parts, model // shards
    bf16, f32 = jnp.bfloat16, jnp.float32
    dma = pltpu.SemaphoreType.DMA
    outs = dict(
        conv_out=jax.ShapeDtypeStruct((mini, width), f32),
        proj_out=jax.ShapeDtypeStruct((small, quarter), f32),
        in_out=jax.ShapeDtypeStruct((big, units), f32),
        out_out=jax.ShapeDtypeStruct((big, units), f32),
    )
    scratch = dict(
        w_out=pltpu.VMEM(w_out.shape, bf16),
        cot=pltpu.VMEM(cot.shape, bf16),
        proj=pltpu.VMEM(proj.shape, bf16),
        w_in=pltpu.VMEM(w_in.shape, bf16),
        spare=pltpu.VMEM((frames, max(units, taps)), bf16),
        conv_weight=pltpu.VMEM(conv_weight.shape, bf16),
        valid=pltpu.VMEM((frames, 1), f32),
        pre_act=pltpu.VMEM((width, frames), f32),
        features=pltpu.VMEM((width, frames), bf16),
        outgoing=pltpu.VMEM((frames, width), bf16),
        arrived=pltpu.VMEM((frames, width), bf16),
        packed=pltpu.VMEM((frames, channels), bf16),
        hid_ln=pltpu.VMEM((frames, model), bf16),
        active=pltpu.VMEM((frames, units), bf16),
        grad_up=pltpu.VMEM((frames, units), bf16),
        normed_part=pltpu.VMEM((frames, model), bf16),
        near_in=pltpu.VMEM((parts, fars * share, model), bf16),
        staged=pltpu.VMEM((parts, fars, share, model), bf16),
        far_in=pltpu.VMEM((parts, fars, share, model), bf16),
        own_sum=pltpu.VMEM((parts, share, model), f32),
        made=pltpu.VMEM((4, model, units // 2), bf16),
        taken=pltpu.VMEM((4, parts, big, units // 2), bf16),
        grad=pltpu.VMEM((parts, share, channels), bf16),
        middle=pltpu.VMEM((parts, rows, width), bf16),
        back=pltpu.VMEM((parts, rows, width), bf16),
        proj_sum=pltpu.VMEM((channels, model), f32),
        proj_term=pltpu.VMEM((channels, model), bf16),
        proj_in=pltpu.VMEM((shards, channels, quarter), bf16),
        proj_made=pltpu.VMEM((channels, quarter), bf16),
        proj_taken=pltpu.VMEM((parts, small, quarter), bf16),
        grad_pre=pltpu.VMEM((width, frames), bf16),
        conv_made=pltpu.VMEM((taps, width), bf16),
        conv_taken=pltpu.VMEM((parts, mini, width), bf16),
        load_sem=dma((10,)),
        keep_sem=dma((parts,)),
        own_sem=dma((2,)),
        dp_send=dma((parts,)),
        dp_recv=dma((parts,)),
        near_send=dma((parts,)),
        near_recv=dma((parts,)),
        sum_near_send=dma((parts,)),
        sum_near_recv=dma((parts,)),
        back_send=dma((parts,)),
        back_recv=dma((parts,)),
        proj_dp_send=dma((parts,)),
        proj_dp_recv=dma((parts,)),
        conv_dp_send=dma((parts,)),
        conv_dp_recv=dma((parts,)),
        far_send=dma((parts, fars)),
        far_recv=dma((parts, fars)),
        pass_send=dma((parts, fars)),
        pass_recv=dma((parts, fars)),
        sum_far_send=dma((parts, fars)),
        sum_far_recv=dma((parts, fars)),
        col_send=dma((shards,)),
        col_recv=dma((shards,)),
        proj_send=dma((shards,)),
        proj_recv=dma((shards,)),
        halve_send=dma((4, parts)),
        halve_recv=dma((4, parts)),
    )
    names = tuple(ins) + tuple(outs) + tuple(scratch)
    vmem = pl.BlockSpec(memory_space=pltpu.VMEM)
    anywhere = pl.BlockSpec(memory_space=pl.ANY)
    return pl.pallas_call(
        functools.partial(step_kernel, parts, shards, names),
        out_shape=list(outs.values()),
        in_specs=[vmem] * vmem_ins + [anywhere] * (len(ins) - vmem_ins),
        out_specs=[vmem] * len(outs),
        scratch_shapes=list(scratch.values()),
        compiler_params=pltpu.CompilerParams(
            collective_id=1, has_side_effects=True, vmem_limit_bytes=VMEM_LIMIT
        ),
        name="step",
    )(*ins.values())


def hand_over_kernel(count, *refs):
    for i in range(count):
        refs[count + i][...] = refs[i][...]


def hand_over(results):
    return pl.pallas_call(
        functools.partial(hand_over_kernel, len(results)),
        out_shape=[jax.ShapeDtypeStruct(value.shape, value.dtype) for value in results],
        name="hand_over",
    )(*results)


def on_device(
    conv_in,
    conv_weight,
    feature_gain,
    proj_weight,
    block_gain,
    w_in,
    w_out,
    cotangent,
    send_index,
    slot_valid,
):
    ins = dict(
        valid_row=slot_valid[None, :], index_row=send_index[None, :],
        gain_feat=feature_gain[None, :], gain_block=block_gain[None, :], conv_in_hbm=conv_in,
        conv_weight_hbm=conv_weight, proj_hbm=proj_weight, w_in_hbm=w_in, w_out_hbm=w_out,
        cot_hbm=cotangent,
    )
    return tuple(hand_over(run_step(ins, 4)))


def solution(mesh):
    placed = (
        P("dp", None),
        P(None, "mp"),
        P(),
        P(),
        P(),
        P(None, "mp"),
        P(None, "mp"),
        P("dp", None),
        P("dp"),
        P("dp"),
    )
    return jax.shard_map(
        on_device,
        mesh=mesh,
        in_specs=placed,
        out_specs=(P("dp", "mp"), P("dp", "mp"), P("dp", "mp"), P("dp", "mp")),
        check_vma=False,
    )
```

```python
import functools
import types

import jax
import jax.numpy as jnp
from jax import lax
from jax.experimental import pallas as pl
from jax.experimental.pallas import tpu as pltpu
from jax.sharding import PartitionSpec as P

EPSILON = 1e-05
SQRT_HALF = 0.7071067811865476
INV_SQRT_TWO_PI = 0.3989422804014327
VMEM_LIMIT = 67043328


def gelu_exact(values):
    return 0.5 * values * (1.0 + lax.erf(values * SQRT_HALF))


def gelu_slope(values):
    return 0.5 * (1.0 + lax.erf(values * SQRT_HALF)) + values * INV_SQRT_TWO_PI * jnp.exp(
        -0.5 * values * values
    )


def normalize(values):
    row_mean = jnp.mean(values, axis=-1, keepdims=True)
    centred = values - row_mean
    inv_std = lax.rsqrt(jnp.mean(centred * centred, axis=-1, keepdims=True) + EPSILON)
    return (centred * inv_std, inv_std)


def norm_back(upstream, normed, inv_std, gain_row):
    scaled = upstream * gain_row
    first_mean = jnp.mean(scaled, axis=-1, keepdims=True)
    second_mean = jnp.mean(scaled * normed, axis=-1, keepdims=True)
    return inv_std * (scaled - first_mean - normed * second_mean)


def contract_rows(left, right):
    return lax.dot_general(
        left, right, (((0,), (0,)), ((), ())), preferred_element_type=jnp.float32
    )


def contract_cols(left, right):
    return lax.dot_general(
        left, right, (((1,), (1,)), ((), ())), preferred_element_type=jnp.float32
    )


def start_copy(src, dst, send_sem, recv_sem, axis, index):
    copy = remote(src, dst, send_sem, recv_sem, axis, index)
    copy.start()
    return copy


def remote(src, dst, send_sem, recv_sem, axis, index):
    return pltpu.make_async_remote_copy(
        src_ref=src,
        dst_ref=dst,
        send_sem=send_sem,
        recv_sem=recv_sem,
        device_id={axis: index},
        device_id_type=pl.DeviceIdType.MESH,
    )


def greet(peers):
    barrier = pltpu.get_barrier_semaphore()
    for axis, index in peers:
        pl.semaphore_signal(
            barrier, inc=1, device_id={axis: index}, device_id_type=pl.DeviceIdType.MESH
        )
    return barrier, len(peers)


def block_of(index, size):
    return pl.ds(pl.multiple_of(index * size, size), size)


def loop(count, body):
    def step(t, carry):
        body(t)
        return carry

    lax.fori_loop(0, count, step, 0)


def step_kernel(parts, shards, names, *refs):
    r = types.SimpleNamespace(**dict(zip(names, refs)))
    outgoing, arrived, packed = r.outgoing, r.arrived, r.packed
    frames, width = outgoing.shape
    rows = frames // parts
    share = rows // shards
    fars = shards // 2
    group_rows = fars * share
    levels = parts.bit_length() - 1
    half = parts // 2
    w_in, w_out, proj, cot = r.w_in, r.w_out, r.proj, r.cot
    spare = r.spare
    d = lax.axis_index("dp")
    m = lax.axis_index("mp")
    side = lax.rem(m, 2)
    line = m // 2
    near = m + 1 - 2 * side
    piece = side * fars + line

    def load(src, dst, k):
        copy = pltpu.make_async_copy(src, dst, r.load_sem.at[k])
        copy.start()
        return copy

    first_frames = r.normed_part
    strips = 4
    strip = frames // strips
    load_weight = load(r.conv_weight_hbm, r.conv_weight, 5)
    load_frames = [
        load(r.conv_in_hbm.at[block_of(t, strip)], first_frames.at[block_of(t, strip)], 6 + t)
        for t in range(strips)
    ]
    load_w_out = load(r.w_out_hbm, w_out, 0)
    load_cot = load(r.cot_hbm, cot, 1)
    load_proj = load(r.proj_hbm, proj, 2)
    load_w_in = load(r.w_in_hbm, w_in, 3)

    def flip(index, bit):
        return index + bit - 2 * bit * lax.rem(index // bit, 2)

    def owner(bits, k):
        total = 0
        for j, bit in enumerate(bits):
            total = total + bit * lax.rem(lax.rem(d // bit, 2) + lax.rem(k // 2**j, 2), 2)
        return total

    def far(j):
        return lax.rem(m + 2 * j, shards)

    peers = greet(
        [("dp", lax.rem(d + o, parts)) for o in range(1, parts)]
        + [("mp", lax.rem(m + o, shards)) for o in range(1, shards)]
    )
    r.valid[...] = jnp.broadcast_to(r.valid_row[...].astype(jnp.float32), (8, frames)).T[:, :1]

    load_weight.wait()
    weight_rows = r.conv_weight[...].T
    for t in range(strips):
        load_frames[t].wait()
        span = pl.ds(t * strip, strip)
        value = contract_cols(weight_rows, first_frames[span, :])
        r.pre_act[:, span] = value
        r.features[:, span] = gelu_exact(value).astype(jnp.bfloat16)

    def exchange(o):
        target = lax.rem(d + o, parts)
        return remote(
            outgoing.at[block_of(target, rows)],
            arrived.at[block_of(d, rows)],
            r.dp_send.at[o],
            r.dp_recv.at[o],
            "dp",
            target,
        )

    def pack(t, size):
        frame = lax.broadcasted_iota(jnp.int32, (frames, size), 0)
        chosen = jnp.where(frame == r.index_row[:, block_of(t, size)], 1.0, 0.0)
        value = jnp.dot(
            r.features[...], chosen.astype(jnp.bfloat16), preferred_element_type=jnp.float32
        )
        outgoing[block_of(t, size), :] = value.T.astype(jnp.bfloat16)

    if rows % 128 == 0:
        pl.semaphore_wait(*peers)

        def pack_and_send(t):
            pack(lax.rem(d + t + 1, parts), rows)

            @pl.when(t < parts - 1)
            def _():
                exchange(t + 1).start()

        loop(parts, pack_and_send)
    else:
        loop(frames // 128, lambda t: pack(t, 128))
        pl.semaphore_wait(*peers)
        for o in range(1, parts):
            exchange(o).start()

    def source_of(o):
        return lax.rem(d - o + parts, parts)

    def place(o):
        return packed.at[block_of(source_of(o), rows), block_of(m, width)]

    def to_far(o, j, block):
        return remote(
            block, place(o), r.far_send.at[o, j], r.far_recv.at[o, j], "mp", far(j)
        )

    def to_near(o, block):
        return remote(block, place(o), r.near_send.at[o], r.near_recv.at[o], "mp", near)

    def keep(o, block):
        return pltpu.make_async_copy(block, place(o), r.keep_sem.at[o])

    def spread(o, block):
        for j in range(1, fars):
            to_far(o, j, block).start()
        to_near(o, block).start()
        keep(o, block).start()

    def relay(o):
        exchange(o).wait_recv()
        spread(o, arrived.at[block_of(source_of(o), rows)])

    def pass_on(o, j):
        col = block_of(lax.rem(m - 2 * j + shards, shards), width)
        part = packed.at[block_of(source_of(o), rows), col]
        return remote(part, part, r.pass_send.at[o, j], r.pass_recv.at[o, j], "mp", near)

    def hand_on(o):
        for j in range(1, fars):
            to_far(o, j, arrived.at[block_of(0, rows)]).wait_recv()
            pass_on(o, j).start()

    spread(0, outgoing.at[block_of(d, rows)])

    load_w_out.wait()
    load_cot.wait()

    lead = 2
    for o in range(1, lead):
        relay(o)
        hand_on(o - 1)
    load_proj.wait()
    load_w_in.wait()

    def sum_near(s):
        return remote(
            r.normed_part.at[pl.ds(s * rows + (1 - side) * group_rows, group_rows)],
            r.near_in.at[s],
            r.sum_near_send.at[s],
            r.sum_near_recv.at[s],
            "mp",
            near,
        )

    def sum_far(s, j):
        return remote(
            r.staged.at[s, j],
            r.far_in.at[s, j],
            r.sum_far_send.at[s, j],
            r.sum_far_recv.at[s, j],
            "mp",
            far(j),
        )

    def pair_sum(s):
        sum_near(s).wait_recv()
        for j in range(fars):
            at = lax.rem(line + j, fars) * share
            mine = r.normed_part[pl.ds(pl.multiple_of(s * rows + side * group_rows + at, share), share), :]
            theirs = r.near_in[s, pl.ds(pl.multiple_of(at, share), share), :]
            total = mine.astype(jnp.float32) + theirs.astype(jnp.float32)
            if j:
                r.staged[s, j] = total.astype(jnp.bfloat16)
                sum_far(s, j).start()
            else:
                r.own_sum[s] = total

    def forward(o):
        s = source_of(o)
        span = block_of(s, rows)

        @pl.when(o + lead < parts)
        def _():
            relay(o + lead)

        @pl.when(o + lead - 1 < parts)
        def _():
            hand_on(o + lead - 1)

        to_near(o, arrived.at[block_of(0, rows)]).wait_recv()
        for j in range(1, fars):
            pass_on(o, j).wait_recv()
        keep(o, arrived.at[block_of(0, rows)]).wait()
        normed, _ = normalize(packed[span, :].astype(jnp.float32))
        scaled = (normed * r.gain_feat[...]).astype(jnp.bfloat16)
        hidden = jnp.dot(scaled, proj[...], preferred_element_type=jnp.float32)
        normed, _ = normalize(hidden)
        r.hid_ln[span, :] = (normed * r.gain_block[...]).astype(jnp.bfloat16)
        lines = r.hid_ln[span, :]
        masked = cot[span, :] * r.valid[span, :].astype(jnp.bfloat16)
        cot[span, :] = masked
        units = w_in.shape[1]
        tile = min(256, units)
        for c in range(units // tile):
            cols = pl.ds(c * tile, tile)
            upward = jnp.dot(lines, w_in[:, cols], preferred_element_type=jnp.float32)
            phi = 0.5 * (1.0 + lax.erf(upward * SQRT_HALF))
            slope = phi + upward * INV_SQRT_TWO_PI * jnp.exp(-0.5 * upward * upward)
            r.active[span, cols] = (upward * phi).astype(jnp.bfloat16)
            grad_active = jnp.dot(masked, w_out[:, cols], preferred_element_type=jnp.float32)
            r.grad_up[span, cols] = (grad_active * slope).astype(jnp.bfloat16)
        r.normed_part[span, :] = contract_cols(r.grad_up[span, :], w_in[...]).astype(
            jnp.bfloat16
        )
        sum_near(s).start()

        @pl.when(o > 0)
        def _():
            pair_sum(source_of(o - 1))

    loop(parts, forward)
    pair_sum(source_of(parts - 1))
    load_conv = load(r.conv_in_hbm, spare, 4)

    natural = [2**j for j in range(levels)]
    swapped = natural[1::-1] + natural[2:]
    big, units = r.out_out.shape
    part = units // 2

    def unit(made, taken, out, bits, send, recv):
        return types.SimpleNamespace(
            made=made, taken=taken, out=out, bits=bits, send=send, recv=recv, size=out.shape[0]
        )

    def big_unit(u, out, bits):
        return unit(
            r.made.at[u], r.taken.at[u], out.at[:, pl.ds(u % 2 * part, part)], bits,
            r.halve_send.at[u], r.halve_recv.at[u],
        )

    out_a = big_unit(0, r.out_out, natural)
    out_b = big_unit(1, r.out_out, swapped)
    in_a = big_unit(2, r.in_out, natural)
    in_b = big_unit(3, r.in_out, natural)
    sides = [(cot, r.active, 0), (cot, r.active, 1), (r.hid_ln, r.grad_up, 0), (r.hid_ln, r.grad_up, 1)]
    bigs = [out_a, out_b, in_a, in_b]
    proj_unit = unit(r.proj_made, r.proj_taken, r.proj_out, natural, r.proj_dp_send, r.proj_dp_recv)
    conv_unit = unit(r.conv_made, r.conv_taken, r.conv_out, natural, r.conv_dp_send, r.conv_dp_recv)

    def halve(x, k, j):
        return remote(
            x.made.at[block_of(owner(x.bits, k), x.size)], x.taken.at[k], x.send.at[k],
            x.recv.at[k], "dp", flip(d, x.bits[j]),
        )

    def make_pair(u, first, second):
        left, right, h = sides[u]
        x = bigs[u]
        a, b = owner(x.bits, first), owner(x.bits, second)
        both = jnp.concatenate([left[:, block_of(a, big)], left[:, block_of(b, big)]], axis=1)
        value = contract_rows(both, right[:, pl.ds(h * part, part)]).astype(jnp.bfloat16)
        x.made[block_of(a, big), :] = value[:big]
        x.made[block_of(b, big), :] = value[big:]

    def make_odd(u, sent):
        x = bigs[u]
        if big % 128:
            left, right, h = sides[u]

            def rows_strip(t):
                x.made[block_of(t, 128), :] = contract_rows(
                    left[:, block_of(t, 128)], right[:, pl.ds(h * part, part)]
                ).astype(jnp.bfloat16)

            loop(left.shape[1] // 128, rows_strip)

        def odd(t):
            first = parts - 1 - 2 * t
            if big % 128 == 0:
                make_pair(u, first, first - half)
            if sent:
                send_pair(x, t)

        loop(parts // 4, odd)

    def send_pair(x, t):
        first = parts - 1 - 2 * t
        halve(x, first, 0).start()
        halve(x, first - half, 0).start()

    def send_pairs(x, start, stop):
        for t in range(start, stop):
            send_pair(x, t)

    def make_even(u):
        if big % 128 == 0:
            loop(parts // 4, lambda t: make_pair(u, parts - 2 - 2 * t, half - 2 - 2 * t))

    def low_bit(k):
        return (k & -k).bit_length() - 1 if k else levels

    def settle(x, k):
        j = low_bit(k)
        base = owner(x.bits, k) * x.size
        for low in range(j):
            halve(x, k + 2**low, low).wait_recv()

        def tile(t):
            span = pl.ds(pl.multiple_of(base + t * 16, 16), 16)
            rows_in = pl.ds(pl.multiple_of(t * 16, 16), 16)
            total = x.made[span, :].astype(jnp.float32)
            for low in range(j):
                total = total + x.taken[k + 2**low, rows_in, :].astype(jnp.float32)
            if k:
                x.made[span, :] = total.astype(jnp.bfloat16)
            else:
                x.out[rows_in, :] = total

        loop(x.size // 16, tile)
        if k:
            halve(x, k, j).start()

    def settle_level(x, j):
        for k in range(parts - 1, 0, -1):
            if low_bit(k) == j:
                settle(x, k)

    def send_first(x):
        for k in range(parts - 1, 0, -2):
            halve(x, k, 0).start()

    quarter_way = max(1, parts // 8)
    make_odd(0, True)
    make_odd(1, True)
    make_odd(2, False)
    send_pairs(in_a, 0, quarter_way)

    per = min(parts, max(1, 256 // share))
    channels = packed.shape[1]

    def back_chain(g):
        sources = [g * per + i for i in range(per)]
        spans = [
            pl.ds(pl.multiple_of(s * rows + piece * share, share), share) for s in sources
        ]

        def rows_of(ref):
            return jnp.concatenate([ref[span, :] for span in spans], axis=0)

        feat_norm, feat_inv = normalize(rows_of(packed).astype(jnp.float32))
        feat_ln = (feat_norm * r.gain_feat[...]).astype(jnp.bfloat16)
        hidden = jnp.dot(feat_ln, proj[...], preferred_element_type=jnp.float32)
        hid_norm, hid_inv = normalize(hidden)
        for s in sources:
            for j in range(1, fars):
                sum_far(s, j).wait_recv()
        upstream = []
        for s in sources:
            total = r.own_sum[s]
            for j in range(1, fars):
                total = total + r.far_in[s, j].astype(jnp.float32)
            upstream.append(total)
        upstream = jnp.concatenate(upstream, axis=0)
        direct = rows_of(cot).astype(jnp.float32)
        grad_hidden = (
            direct + norm_back(upstream, hid_norm, hid_inv, r.gain_block[...])
        ).astype(jnp.bfloat16)
        grad_feat = contract_cols(grad_hidden, proj[...])
        grad_packed = norm_back(grad_feat, feat_norm, feat_inv, r.gain_feat[...]).astype(
            jnp.bfloat16
        )
        for i, s in enumerate(sources):
            r.grad[s] = grad_packed[i * share : (i + 1) * share]
        term = contract_rows(feat_ln, grad_hidden)
        proj_sum = r.proj_sum

        @pl.when(g == 0)
        def _():
            proj_sum[...] = term

        @pl.when(g > 0)
        def _():
            proj_sum[...] = proj_sum[...] + term

    loop(parts // per, back_chain)

    def columns(o):
        peer = lax.rem(m + o, shards)
        return remote(
            r.grad.at[:, :, block_of(peer, width)],
            r.middle.at[:, block_of(piece, share), :],
            r.col_send.at[o],
            r.col_recv.at[o],
            "mp",
            peer,
        )

    for o in range(1, shards):
        columns(o).start()
    own_columns = pltpu.make_async_copy(
        r.grad.at[:, :, block_of(m, width)],
        r.middle.at[:, block_of(piece, share), :],
        r.own_sem.at[0],
    )
    own_columns.start()
    quarter = r.proj_out.shape[1]
    r.proj_term[...] = r.proj_sum[...].astype(jnp.bfloat16)

    def proj_columns(o):
        peer = lax.rem(m + o, shards)
        return remote(
            r.proj_term.at[:, block_of(peer, quarter)],
            r.proj_in.at[o],
            r.proj_send.at[o],
            r.proj_recv.at[o],
            "mp",
            peer,
        )

    for o in range(1, shards):
        proj_columns(o).start()

    make_even(0)
    settle_level(out_a, 1)
    make_even(1)
    make_odd(3, False)
    make_even(2)
    make_even(3)
    for o in range(1, shards):
        columns(o).wait_recv()
    own_columns.wait()

    def give_back(o):
        target = lax.rem(d + o, parts)
        return remote(
            r.middle.at[target],
            r.back.at[d],
            r.back_send.at[o],
            r.back_recv.at[o],
            "dp",
            target,
        )

    for o in range(1, parts):
        give_back(o).start()
    own_block = pltpu.make_async_copy(r.middle.at[d], r.back.at[d], r.own_sem.at[1])
    own_block.start()

    settle_level(out_b, 1)
    send_pairs(in_a, quarter_way, parts // 4)
    send_pairs(in_b, 0, quarter_way)
    settle_level(in_a, 1)
    for j in range(2, levels):
        settle_level(out_a, j)

    for o in range(1, shards):
        proj_columns(o).wait_recv()
    proj_total = r.proj_term[:, block_of(m, quarter)].astype(jnp.float32)
    for o in range(1, shards):
        proj_total = proj_total + r.proj_in[o].astype(jnp.float32)
    r.proj_made[...] = proj_total.astype(jnp.bfloat16)

    send_first(proj_unit)

    for o in range(1, parts):
        give_back(o).wait_recv()
    own_block.wait()
    load_conv.wait()
    for j in range(2, levels):
        settle_level(out_b, j)
    returned = jnp.concatenate([r.back[e] for e in range(parts)], axis=0).T
    tile = min(256, frames)

    def conv_back(t):
        span = block_of(t, tile)
        frame = t * tile + lax.broadcasted_iota(jnp.int32, (tile, frames), 0)
        chosen = jnp.where(frame == r.index_row[...], 1.0, 0.0).astype(jnp.bfloat16)
        grad_features = contract_cols(returned, chosen)
        r.grad_pre[:, span] = (grad_features * gelu_slope(r.pre_act[:, span])).astype(jnp.bfloat16)

    loop(frames // tile, conv_back)
    conv_term = jnp.dot(r.grad_pre[...], spare[...], preferred_element_type=jnp.float32)
    r.conv_made[...] = conv_term.T.astype(jnp.bfloat16)
    send_first(conv_unit)
    send_pairs(in_b, quarter_way, parts // 4)

    for j in range(2, levels):
        settle_level(in_a, j)
    settle_level(proj_unit, 1)
    settle_level(in_b, 1)
    settle_level(conv_unit, 1)
    settle(out_a, 0)
    settle(out_b, 0)
    for j in range(2, levels):
        settle_level(in_b, j)
        settle_level(proj_unit, j)
        settle_level(conv_unit, j)
    settle(in_a, 0)
    settle(proj_unit, 0)
    settle(conv_unit, 0)
    settle(in_b, 0)

    for o in range(1, parts):
        exchange(o).wait_send()
        give_back(o).wait_send()

    def drain(o):
        block = arrived.at[block_of(0, rows)]
        to_near(o, block).wait_send()
        sum_near(o).wait_send()
        for j in range(1, fars):
            to_far(o, j, block).wait_send()
            pass_on(o, j).wait_send()
            sum_far(o, j).wait_send()

    loop(parts, drain)
    for o in range(1, shards):
        columns(o).wait_send()
        proj_columns(o).wait_send()
    for x in bigs + [proj_unit, conv_unit]:
        for k in range(1, parts):
            halve(x, k, low_bit(k)).wait_send()


def run_step(ins, vmem_ins):
    parts, shards = lax.axis_size("dp"), lax.axis_size("mp")
    conv_in, conv_weight, proj, w_in, w_out, cot = list(ins.values())[vmem_ins:]
    frames, width = conv_in.shape[0], conv_weight.shape[1]
    rows = frames // parts
    share = rows // shards
    fars = max(shards // 2, 1)
    channels, model = proj.shape
    units = w_in.shape[1]
    taps = conv_in.shape[1]
    big, small, mini, quarter = model // parts, channels // parts, taps // parts, model // shards
    bf16, f32 = jnp.bfloat16, jnp.float32
    dma = pltpu.SemaphoreType.DMA
    outs = dict(
        conv_out=jax.ShapeDtypeStruct((mini, width), f32),
        proj_out=jax.ShapeDtypeStruct((small, quarter), f32),
        in_out=jax.ShapeDtypeStruct((big, units), f32),
        out_out=jax.ShapeDtypeStruct((big, units), f32),
    )
    scratch = dict(
        w_out=pltpu.VMEM(w_out.shape, bf16),
        cot=pltpu.VMEM(cot.shape, bf16),
        proj=pltpu.VMEM(proj.shape, bf16),
        w_in=pltpu.VMEM(w_in.shape, bf16),
        spare=pltpu.VMEM((frames, max(units, taps)), bf16),
        conv_weight=pltpu.VMEM(conv_weight.shape, bf16),
        valid=pltpu.VMEM((frames, 1), f32),
        pre_act=pltpu.VMEM((width, frames), f32),
        features=pltpu.VMEM((width, frames), bf16),
        outgoing=pltpu.VMEM((frames, width), bf16),
        arrived=pltpu.VMEM((frames, width), bf16),
        packed=pltpu.VMEM((frames, channels), bf16),
        hid_ln=pltpu.VMEM((frames, model), bf16),
        active=pltpu.VMEM((frames, units), bf16),
        grad_up=pltpu.VMEM((frames, units), bf16),
        normed_part=pltpu.VMEM((frames, model), bf16),
        near_in=pltpu.VMEM((parts, fars * share, model), bf16),
        staged=pltpu.VMEM((parts, fars, share, model), bf16),
        far_in=pltpu.VMEM((parts, fars, share, model), bf16),
        own_sum=pltpu.VMEM((parts, share, model), f32),
        made=pltpu.VMEM((4, model, units // 2), bf16),
        taken=pltpu.VMEM((4, parts, big, units // 2), bf16),
        grad=pltpu.VMEM((parts, share, channels), bf16),
        middle=pltpu.VMEM((parts, rows, width), bf16),
        back=pltpu.VMEM((parts, rows, width), bf16),
        proj_sum=pltpu.VMEM((channels, model), f32),
        proj_term=pltpu.VMEM((channels, model), bf16),
        proj_in=pltpu.VMEM((shards, channels, quarter), bf16),
        proj_made=pltpu.VMEM((channels, quarter), bf16),
        proj_taken=pltpu.VMEM((parts, small, quarter), bf16),
        grad_pre=pltpu.VMEM((width, frames), bf16),
        conv_made=pltpu.VMEM((taps, width), bf16),
        conv_taken=pltpu.VMEM((parts, mini, width), bf16),
        load_sem=dma((10,)),
        keep_sem=dma((parts,)),
        own_sem=dma((2,)),
        dp_send=dma((parts,)),
        dp_recv=dma((parts,)),
        near_send=dma((parts,)),
        near_recv=dma((parts,)),
        sum_near_send=dma((parts,)),
        sum_near_recv=dma((parts,)),
        back_send=dma((parts,)),
        back_recv=dma((parts,)),
        proj_dp_send=dma((parts,)),
        proj_dp_recv=dma((parts,)),
        conv_dp_send=dma((parts,)),
        conv_dp_recv=dma((parts,)),
        far_send=dma((parts, fars)),
        far_recv=dma((parts, fars)),
        pass_send=dma((parts, fars)),
        pass_recv=dma((parts, fars)),
        sum_far_send=dma((parts, fars)),
        sum_far_recv=dma((parts, fars)),
        col_send=dma((shards,)),
        col_recv=dma((shards,)),
        proj_send=dma((shards,)),
        proj_recv=dma((shards,)),
        halve_send=dma((4, parts)),
        halve_recv=dma((4, parts)),
    )
    names = tuple(ins) + tuple(outs) + tuple(scratch)
    vmem = pl.BlockSpec(memory_space=pltpu.VMEM)
    anywhere = pl.BlockSpec(memory_space=pl.ANY)
    return pl.pallas_call(
        functools.partial(step_kernel, parts, shards, names),
        out_shape=list(outs.values()),
        in_specs=[vmem] * vmem_ins + [anywhere] * (len(ins) - vmem_ins),
        out_specs=[vmem] * len(outs),
        scratch_shapes=list(scratch.values()),
        compiler_params=pltpu.CompilerParams(
            collective_id=1, has_side_effects=True, vmem_limit_bytes=VMEM_LIMIT
        ),
        name="step",
    )(*ins.values())


def hand_over_kernel(count, *refs):
    for i in range(count):
        refs[count + i][...] = refs[i][...]


def hand_over(results):
    return pl.pallas_call(
        functools.partial(hand_over_kernel, len(results)),
        out_shape=[jax.ShapeDtypeStruct(value.shape, value.dtype) for value in results],
        name="hand_over",
    )(*results)


def on_device(
    conv_in,
    conv_weight,
    feature_gain,
    proj_weight,
    block_gain,
    w_in,
    w_out,
    cotangent,
    send_index,
    slot_valid,
):
    ins = dict(
        valid_row=slot_valid[None, :], index_row=send_index[None, :],
        gain_feat=feature_gain[None, :], gain_block=block_gain[None, :], conv_in_hbm=conv_in,
        conv_weight_hbm=conv_weight, proj_hbm=proj_weight, w_in_hbm=w_in, w_out_hbm=w_out,
        cot_hbm=cotangent,
    )
    return tuple(hand_over(run_step(ins, 4)))


def solution(mesh):
    placed = (
        P("dp", None),
        P(None, "mp"),
        P(),
        P(),
        P(),
        P(None, "mp"),
        P(None, "mp"),
        P("dp", None),
        P("dp"),
        P("dp"),
    )
    return jax.shard_map(
        on_device,
        mesh=mesh,
        in_specs=placed,
        out_specs=(P("dp", "mp"), P("dp", "mp"), P("dp", "mp"), P("dp", "mp")),
        check_vma=False,
    )
```
